256 devices in a mesh: tmpl: 32 (over x, z_lo, core), tm: 8 (over y, z_hi).
Axes of the slice: x: 4, y: 4, z: 8 (z_hi: 2, z_lo: 4; z = z_hi * 4 + z_lo), core: 2. Of those that a mesh axis runs over, the one named last changes fastest.
Arguments:
- records: bfloat16 [1536, 4096], P('tmpl', 'tm'), may hold values from -6 to 6
- templates: bfloat16 [2, 1024, 48, 200], P(None, 'tmpl'), may hold values from -0.0625 to 0.0625
- channels: int32 [2, 1024, 48], P(None, 'tmpl'), may hold values from 0 to 1535
- moveouts: int32 [2, 1024, 48], P(None, 'tmpl'), may hold values from 0 to 55
Outputs:
- detections: float32 [2, 1024, 4096], P(None, 'tmpl', 'tm')
The draws below stay inside these ranges and needn't reach their ends.
All inputs are finite; a program needn't handle non-finite values.
Results may differ from the reference program's by a relative error of at most 0.0043.
Values may be sent and summed in bfloat16 or wider, within the bound.
No kernel may reach another device: no remote copies, remote signals or barrier semaphores. Data moves between devices by JAX's collectives and lax.ppermute only.
A program may use at most 64 MiB of HBM per device.

```python
import math
import jax
import jax.numpy as jnp
from jax import lax

C = 1536
K = 48
L = 200
LAGS = 56
BATCHES = 2
NT_DEV = 32
TIME_DEV = 512
NT = 1024
TIME = 4096
N_TMPL = 32
N_TM = 8


def plant(entries, stream_key, least, high):
    dims = entries.shape
    place = [jax.random.randint(jax.random.fold_in(stream_key, axis), (), 0, dims[axis]) for axis in range(len(dims))]
    entries = entries.at[tuple(place)].set(least)
    longest = dims.index(max(dims))
    place[longest] = (place[longest] + 1) % dims[longest]
    return entries.at[tuple(place)].set(high)


def steps_of(own_key, dims, shards, least, largest):
    def one(position, parts):
        draws = jax.random.uniform(jax.random.fold_in(jax.random.fold_in(own_key, 6), position), (parts,), jnp.float32, least / len(shards), largest / len(shards))
        return jnp.repeat(jnp.exp(draws), dims[position] // parts).reshape((-1,) + (1,) * (len(dims) - position - 1))

    factor_of = one(*shards[0])
    for cut in shards[1:]:
        factor_of = factor_of * one(*cut)
    return factor_of


def gaussian(stream_key, extent, spread, limit, pieces=(), kind=jnp.bfloat16):
    values = spread * jax.random.normal(stream_key, extent, jnp.float32)
    if pieces:
        values = values * steps_of(stream_key, extent, pieces, -0.22, 0.18)
    return jnp.clip(values, -limit, limit).astype(kind)


def setup_inputs(seed: int = 0) -> dict:
    splits = jax.random.split(jax.random.key(seed), 5)
    records = gaussian(splits[0], (C, TIME), 1.0, 6.0, ((0, 32), (1, 8)))
    templates = gaussian(splits[1], (BATCHES, NT, K, L), (K * L) ** -0.5, 0.0625, ((1, 32),))
    channels = plant(jax.random.randint(splits[2], (BATCHES, NT, K), 0, C), jax.random.fold_in(splits[2], 1), 0, C - 1).astype(jnp.int32)
    moveouts = plant(jax.random.randint(splits[3], (BATCHES, NT, K), 0, LAGS), jax.random.fold_in(splits[3], 1), 0, LAGS - 1).astype(jnp.int32)
    return {"records": records, "templates": templates, "channels": channels, "moveouts": moveouts}


def tables(count, freqs, width):
    sample = jnp.arange(count, dtype=jnp.int32)[:, None]
    freq = jnp.arange(freqs, dtype=jnp.int32)[None, :]
    angle = (2.0 * math.pi / width) * ((sample * freq) % width).astype(jnp.float32)
    return jnp.concatenate([jnp.cos(angle), jnp.sin(angle)], axis=1)


def reference(records, templates, channels, moveouts):
    width = TIME_DEV + L + LAGS - 2
    freqs = width // 2 + 1
    extra = width - TIME_DEV
    forward = tables(width, freqs, width).astype(jnp.bfloat16)
    inverse = tables(TIME_DEV, freqs, width)
    freq = jnp.arange(freqs, dtype=jnp.int32)
    weight = jnp.where((freq == 0) | (freq == freqs - 1), 1.0, 2.0).astype(jnp.float32) / width
    padded = jnp.pad(records, ((0, 0), (0, extra)))

    def window_spectra(index):
        piece = lax.dynamic_slice_in_dim(padded, (index * TIME_DEV).astype(jnp.int32), width, 1)
        return jnp.dot(piece, forward, preferred_element_type=jnp.float32).astype(jnp.bfloat16)

    spectra = lax.map(window_spectra, jnp.arange(N_TM, dtype=jnp.int32))

    def block(packed):
        waves, chans, lags = packed
        hspec = jnp.dot(waves.reshape(-1, L), forward[:L], preferred_element_type=jnp.float32)
        h_cos, h_sin = hspec[:, :freqs], hspec[:, freqs:]
        angle = (2.0 * math.pi / width) * ((lags.reshape(-1)[:, None] * freq[None, :]) % width).astype(jnp.float32)
        c_theta, s_theta = jnp.cos(angle), jnp.sin(angle)
        rows = chans.reshape(-1)

        def per_window(spec):
            picked = spec[rows].astype(jnp.float32)
            x_cos, x_sin = picked[:, :freqs], picked[:, freqs:]
            prod_a = h_cos * x_cos + h_sin * x_sin
            prod_b = h_sin * x_cos - h_cos * x_sin
            real_part = (prod_a * c_theta - prod_b * s_theta).reshape(NT_DEV, K, freqs).sum(axis=1)
            imag_part = (prod_a * s_theta + prod_b * c_theta).reshape(NT_DEV, K, freqs).sum(axis=1)
            joint = jnp.concatenate([real_part * weight, -imag_part * weight], axis=1)
            return lax.dot_general(joint, inverse, (((1,), (1,)), ((), ())), precision=lax.Precision.HIGHEST)

        outs = lax.map(per_window, spectra)
        return jnp.transpose(outs, (1, 0, 2)).reshape(NT_DEV, N_TM * TIME_DEV)

    blocks = N_TMPL * templates.shape[0]
    waves = templates.reshape(blocks, NT_DEV, K, L)
    chans = channels.reshape(blocks, NT_DEV, K)
    lags = moveouts.reshape(blocks, NT_DEV, K)
    result = lax.map(block, (waves, chans, lags))
    return result.reshape(templates.shape[0], NT_DEV * N_TMPL, N_TM * TIME_DEV)
```

```python
import functools
import math

import jax
import jax.numpy as jnp
import numpy as np
from jax import lax
from jax.experimental import pallas as pl
from jax.experimental.pallas import tpu as pltpu
from jax.sharding import PartitionSpec as P

L = 200
LAGS = 56
EXTRA = L + LAGS - 2
HOLD = 128


def angles(samples, freqs, width):
    return 2.0 * math.pi / width * (samples[:, None] * freqs[None, :] % width)


def host_tables(time_dev):
    width = time_dev + EXTRA
    freqs = width // 2 + 1
    freq = np.arange(freqs)
    ang = angles(np.arange(time_dev), freq, width)
    forward = np.concatenate([np.cos(ang), np.sin(ang)], axis=1).astype(np.float32).astype(jnp.bfloat16)
    turn = angles(np.arange(LAGS), freq, width)
    cos, sin = (f(turn).reshape(LAGS, freqs // HOLD, HOLD) for f in (np.cos, np.sin))
    phase = np.zeros((LAGS, 16, HOLD), np.float32)
    phase[:, 0:3], phase[:, 4:7] = cos, cos
    phase[:, 8:11], phase[:, 12:15] = -sin, sin
    weight = np.where((freq == 0) | (freq == freqs - 1), 1.0, 2.0) / width
    early = np.arange(time_dev // 2, time_dev) + EXTRA
    tau = np.concatenate([np.arange(time_dev), early])
    back = angles(tau, freq, width)
    inverse = np.concatenate([np.cos(back) * weight, np.sin(back) * weight], axis=1)
    inverse[time_dev:][early < time_dev] = 0.0
    inverse = inverse.T.astype(np.float32)
    high = inverse.astype(jnp.bfloat16)
    low = (inverse - high.astype(np.float32)).astype(jnp.bfloat16)
    return forward, phase.reshape(LAGS * 16, HOLD), high, low


def template_kernel(rows, freqs, lag_ref, wave_ref, forward_ref, phase_ref, out_ref, spec, swap):
    chunks = freqs // HOLD

    @pl.when(pl.program_id(0) == 0)
    def _():
        for pad in (chunks, 4 + chunks):
            spec[pl.ds(pad, rows, stride=8), :] = jnp.zeros((rows, HOLD), jnp.float32)
            swap[pl.ds(pad, rows, stride=8), :] = jnp.zeros((rows, HOLD), jnp.float32)

    dft = jnp.dot(wave_ref[...], forward_ref[...], preferred_element_type=jnp.float32)
    for j in range(chunks):
        real = dft[:, j * HOLD : (j + 1) * HOLD]
        imag = dft[:, freqs + j * HOLD : freqs + (j + 1) * HOLD]
        spec[pl.ds(j, rows, stride=8), :] = real
        spec[pl.ds(4 + j, rows, stride=8), :] = imag
        swap[pl.ds(j, rows, stride=8), :] = imag
        swap[pl.ds(4 + j, rows, stride=8), :] = real
    base = pl.program_id(0) * rows

    def group(g, carry):
        for u in range(8):
            row = g * 8 + u
            lag = pl.multiple_of(lag_ref[base + row], 16)
            at = pl.ds(pl.multiple_of(row * 8, 8), 8)
            out_ref[at, :] = spec[at, :] * phase_ref[pl.ds(lag, 8), :] + swap[at, :] * phase_ref[pl.ds(lag + 8, 8), :]
        return carry

    lax.fori_loop(0, rows // 8, group, 0)


def template_spectra(waves, lags, forward, phase, freqs, rows):
    count, length = waves.shape
    grid = pltpu.PrefetchScalarGridSpec(
        num_scalar_prefetch=1,
        grid=(count // rows,),
        in_specs=[
            pl.BlockSpec((rows, length), lambda i, lag: (i, 0)),
            pl.BlockSpec((length, 2 * freqs), lambda i, lag: (0, 0)),
            pl.BlockSpec(phase.shape, lambda i, lag: (0, 0)),
        ],
        out_specs=pl.BlockSpec((rows * 8, HOLD), lambda i, lag: (i, 0)),
        scratch_shapes=[pltpu.VMEM((rows * 8, HOLD), jnp.float32)] * 2,
    )
    return pl.pallas_call(
        functools.partial(template_kernel, rows, freqs),
        grid_spec=grid,
        out_shape=jax.ShapeDtypeStruct((count * 8, HOLD), jnp.float32),
        compiler_params=pltpu.CompilerParams(vmem_limit_bytes=20 << 20),
        cost_estimate=pl.CostEstimate(flops=count * length * freqs * 4, bytes_accessed=count * 8 * HOLD * 4, transcendentals=0),
        name="template_spectra",
    )(lags, waves, forward[:length], phase)


def detect_kernel(n_blocks, count, stations, freqs, groups, slot_ref, *refs):
    blocks, (forward_ref, high_ref, low_ref, q_hbm, main_ref, early_ref, table, q, acc, sems) = refs[:n_blocks], refs[n_blocks:]
    chunks = freqs // HOLD
    share = count // groups
    span = share * stations * 8
    loads = [pltpu.make_async_copy(q_hbm.at[pl.ds(g * span, span)], q.at[pl.ds(g * span, span)], sems.at[g]) for g in range(groups)]
    for load in loads:
        load.start()
    size = blocks[0].shape[0]
    for b, block in enumerate(blocks):
        dft = jnp.dot(block[...], forward_ref[...], preferred_element_type=jnp.float32)
        for j in range(chunks):
            real = dft[:, j * HOLD : (j + 1) * HOLD]
            imag = dft[:, freqs + j * HOLD : freqs + (j + 1) * HOLD]
            start = b * size * 16
            table[pl.ds(start + j, size, stride=16), :] = real
            table[pl.ds(start + 4 + j, size, stride=16), :] = imag
            table[pl.ds(start + 8 + j, size, stride=16), :] = imag
            table[pl.ds(start + 12 + j, size, stride=16), :] = -real

    def one(t, carry):
        first = second = jnp.zeros((8, HOLD), jnp.float32)
        for k in range(stations):
            row = t * stations + k
            slot = pl.multiple_of(slot_ref[row], 16)
            weight = q[pl.ds(pl.multiple_of(row * 8, 8), 8), :]
            first += weight * table[pl.ds(slot, 8), :]
            second += weight * table[pl.ds(slot + 8, 8), :]
        acc[pl.ds(pl.multiple_of(t * 16, 16), 8), :] = first
        acc[pl.ds(pl.multiple_of(t * 16 + 8, 8), 8), :] = second
        return carry

    for g, load in enumerate(loads):
        load.wait()
        lax.fori_loop(g * share, (g + 1) * share, one, 0)
    joint = jnp.concatenate(
        [
            acc[pl.ds(8 * part + j, count, stride=16), :] + acc[pl.ds(8 * part + 4 + j, count, stride=16), :]
            for part in range(2)
            for j in range(chunks)
        ],
        axis=1,
    )
    top = joint.astype(jnp.bfloat16)
    rest = (joint - top.astype(jnp.float32)).astype(jnp.bfloat16)
    out = (
        jnp.dot(top, high_ref[...], preferred_element_type=jnp.float32)
        + jnp.dot(rest, high_ref[...], preferred_element_type=jnp.float32)
        + jnp.dot(top, low_ref[...], preferred_element_type=jnp.float32)
    )
    time_dev = main_ref.shape[1]
    main_ref[...] = out[:, :time_dev]
    early_ref[...] = out[:, time_dev:]


def detect(slots, blocks, forward, high, low, q, count, stations, freqs, time_dev):
    groups = 8
    rows = sum(b.shape[0] for b in blocks)
    whole = pl.BlockSpec(memory_space=pltpu.VMEM)
    return pl.pallas_call(
        functools.partial(detect_kernel, len(blocks), count, stations, freqs, groups),
        in_specs=[pl.BlockSpec(memory_space=pltpu.SMEM)] + [whole] * (len(blocks) + 3) + [pl.BlockSpec(memory_space=pl.ANY)],
        out_specs=[whole, whole],
        out_shape=[
            jax.ShapeDtypeStruct((count, time_dev), jnp.float32),
            jax.ShapeDtypeStruct((count, time_dev // 2), jnp.float32),
        ],
        scratch_shapes=[
            pltpu.VMEM((rows * 16, HOLD), jnp.float32),
            pltpu.VMEM((count * stations * 8, HOLD), jnp.float32),
            pltpu.VMEM((count * 16, HOLD), jnp.float32),
            pltpu.SemaphoreType.DMA((groups,)),
        ],
        compiler_params=pltpu.CompilerParams(vmem_limit_bytes=40 << 20),
        cost_estimate=pl.CostEstimate(flops=rows * time_dev * freqs * 4, bytes_accessed=count * stations * 8 * HOLD * 4, transcendentals=0),
        name="detect",
    )(slots, *blocks, forward, high, low, q)


def route(change):
    dx, dz, dc = change
    code = (dx * 4 + dz) * 2 + dc
    return [(i, i ^ code) for i in range(32)]


def per_device(records, templates, channels, moveouts):
    per, time_dev = records.shape
    batches, count, stations, length = templates.shape
    freqs = (time_dev + EXTRA) // 2 + 1
    forward, phase, high, low = (jnp.asarray(t) for t in host_tables(time_dev))
    swap = lambda block, change: lax.ppermute(block, "tmpl", route(change))

    line = jnp.concatenate([records] + [swap(records, (0, d, 0)) for d in (1, 2, 3)], axis=0)
    plane = [line] + [swap(line, (d, 0, 0)) for d in (1, 2, 3)]
    blocks = plane + [swap(block, (0, 0, 1)) for block in plane]

    apart = (channels // per) ^ lax.axis_index("tmpl")
    place = ((apart & 1) * 16 + (apart >> 1)) * per + channels % per
    slots = (place * 16).reshape(-1)

    q = template_spectra(
        templates.reshape(-1, length), (moveouts * 16).reshape(-1), forward, phase, freqs, 384
    )
    main, early = detect(slots, blocks, forward, high, low, q, batches * count, stations, freqs, time_dev)
    earlier = lax.ppermute(early, "tm", [(i, i - 1) for i in range(1, lax.axis_size("tm"))])
    out = main + jnp.pad(earlier, ((0, 0), (time_dev - earlier.shape[1], 0)))
    return out.reshape(batches, count, time_dev)


def solution(mesh):
    placed = (
        P("tmpl", "tm"),
        P(None, "tmpl", None, None),
        P(None, "tmpl", None),
        P(None, "tmpl", None),
    )
    return jax.shard_map(
        per_device, mesh=mesh, in_specs=placed, out_specs=P(None, "tmpl", "tm"), check_vma=False
    )
```

```python
import functools
import math

import jax
import jax.numpy as jnp
import numpy as np
from jax import lax
from jax.experimental import pallas as pl
from jax.experimental.pallas import tpu as pltpu
from jax.sharding import PartitionSpec as P

L = 200
LAGS = 56
EXTRA = L + LAGS - 2
HOLD = 128
LAG_ROWS = 64
VMEM_K1 = 20 << 20
VMEM_K2 = 34 << 20
GROUPS = 8


def angles(samples, freqs, width):
    return 2.0 * math.pi / width * (samples[:, None] * freqs[None, :] % width)


def host_tables(time_dev):
    width = time_dev + EXTRA
    freqs = width // 2 + 1
    freq = np.arange(freqs)
    ang = angles(np.arange(time_dev), freq, width)
    forward = np.concatenate([np.cos(ang), np.sin(ang)], axis=1).astype(np.float32).astype(jnp.bfloat16)
    turn = angles(np.arange(LAGS), freq, width)
    phase = np.zeros((2 * LAG_ROWS, 2 * freqs), jnp.bfloat16)
    phase[:LAGS], phase[LAG_ROWS : LAG_ROWS + LAGS] = halves(np.concatenate([np.cos(turn), np.sin(turn)], axis=1))
    weight = np.where((freq == 0) | (freq == freqs - 1), 1.0, 2.0) / width
    early = np.arange(time_dev // 2, time_dev) + EXTRA
    tau = np.concatenate([np.arange(time_dev), early])
    back = angles(tau, freq, width)
    inverse = np.concatenate([np.cos(back) * weight, np.sin(back) * weight], axis=1)
    inverse[time_dev:][early < time_dev] = 0.0
    return forward, phase, *halves(inverse.T)


def halves(table):
    table = table.astype(np.float32)
    high = table.astype(jnp.bfloat16)
    return high, (table - high.astype(np.float32)).astype(jnp.bfloat16)


def template_kernel(step, freqs, lag_ref, record_ref, wave_hbm, forward_hbm, phase_hbm, out_hbm, own_ref, waves, forward, phases, out, sems, out_sems):
    starts = range(0, wave_hbm.shape[0], step)
    loads = [pltpu.make_async_copy(forward_hbm, forward, sems.at[0]), pltpu.make_async_copy(phase_hbm, phases, sems.at[1])]
    for n, start in enumerate(starts):
        part = pl.ds(start, step)
        loads.append(pltpu.make_async_copy(wave_hbm.at[part], waves.at[part], sems.at[2 + n]))
    for load in loads:
        load.start()
    own_ref[...] = record_ref[...]
    stores = []
    for n, start in enumerate(starts):
        for load in loads[:3] if n == 0 else loads[2 + n : 3 + n]:
            load.wait()
        lag = jnp.concatenate([lag_ref[pl.ds((start + at) // HOLD, 1), :] for at in range(0, step, HOLD)], axis=1)
        lag_row = lax.broadcasted_iota(jnp.int32, (2 * LAG_ROWS, step), 0) & (LAG_ROWS - 1)
        chosen = (lag_row == lag).astype(jnp.float32).astype(jnp.bfloat16)
        phase = lax.dot_general(chosen, phases[...], (((0,), (0,)), ((), ())), preferred_element_type=jnp.float32)
        dft = jnp.dot(waves[pl.ds(start, step), :], forward[...], preferred_element_type=jnp.float32)
        for j in range(freqs // HOLD):
            low, high = slice(j * HOLD, (j + 1) * HOLD), slice(freqs + j * HOLD, freqs + (j + 1) * HOLD)
            h_cos, h_sin, c_theta, s_theta = dft[:, low], dft[:, high], phase[:, low], phase[:, high]
            out[pl.ds(start * 8 + j, step, stride=8), :] = h_cos * c_theta - h_sin * s_theta
            out[pl.ds(start * 8 + 4 + j, step, stride=8), :] = h_cos * s_theta + h_sin * c_theta
        part = pl.ds(start * 8, step * 8)
        stores.append(pltpu.make_async_copy(out.at[part], out_hbm.at[part], out_sems.at[n]))
        stores[-1].start()
    for store in stores:
        store.wait()


def template_spectra(waves, lags, records, forward, phase, freqs):
    count, length = waves.shape
    whole = pl.BlockSpec(memory_space=pltpu.VMEM)
    step = 512
    return pl.pallas_call(
        functools.partial(template_kernel, step, freqs),
        in_specs=[whole] * 2 + [pl.BlockSpec(memory_space=pltpu.HBM)] * 3,
        out_specs=[pl.BlockSpec(memory_space=pltpu.HBM), whole],
        out_shape=[pltpu.HBM((count * 8, HOLD), jnp.float32), jax.ShapeDtypeStruct(records.shape, records.dtype)],
        scratch_shapes=[
            pltpu.VMEM(waves.shape, waves.dtype),
            pltpu.VMEM((length, 2 * freqs), forward.dtype),
            pltpu.VMEM(phase.shape, phase.dtype),
            pltpu.VMEM((count * 8, HOLD), jnp.float32),
            pltpu.SemaphoreType.DMA((2 + count // step,)),
            pltpu.SemaphoreType.DMA((count // step,)),
        ],
        compiler_params=pltpu.CompilerParams(vmem_limit_bytes=VMEM_K1),
        cost_estimate=pl.CostEstimate(flops=count * length * freqs * 4, bytes_accessed=count * 8 * HOLD * 4, transcendentals=0),
        name="template_spectra",
    )(lags, records, *(pltpu.with_memory_space_constraint(a, pltpu.HBM) for a in (waves, forward[:length], phase)))


def detect_kernel(n_blocks, count, stations, freqs, slot_ref, *refs):
    blocks, (q_hbm, forward_ref, high_ref, low_ref, main_ref, early_ref, table, acc, q, sems) = refs[:n_blocks], refs[n_blocks:]
    share = count // GROUPS
    loads = []
    for g in range(GROUPS):
        part = pl.ds(g * share * stations * 8, share * stations * 8)
        loads.append(pltpu.make_async_copy(q_hbm.at[part], q.at[part], sems.at[g]))
        loads[g].start()
    chunks = freqs // HOLD
    size = blocks[0].shape[0]
    for b, block in enumerate(blocks):
        dft = jnp.dot(block[...], forward_ref[...], preferred_element_type=jnp.float32)
        for j in range(chunks):
            real = dft[:, j * HOLD : (j + 1) * HOLD]
            imag = dft[:, freqs + j * HOLD : freqs + (j + 1) * HOLD]
            start = b * size * 16
            table[pl.ds(start + j, size, stride=16), :] = real
            table[pl.ds(start + 4 + j, size, stride=16), :] = imag
            table[pl.ds(start + 8 + j, size, stride=16), :] = imag
            table[pl.ds(start + 12 + j, size, stride=16), :] = -real

    def one(t, carry):
        first = [jnp.zeros((8, HOLD), jnp.float32)] * 2
        second = list(first)
        weights = q.at[pl.ds(pl.multiple_of(t * stations * 8, stations * 8), stations * 8), :]
        for k in range(stations):
            slot = pl.multiple_of(slot_ref[t, k], 16)
            weight = weights[k * 8 : k * 8 + 8, :]
            first[k % 2] += weight * table[pl.ds(slot, 8), :]
            second[k % 2] += weight * table[pl.ds(slot + 8, 8), :]
        acc[pl.ds(pl.multiple_of(t * 16, 16), 8), :] = first[0] + first[1]
        acc[pl.ds(pl.multiple_of(t * 16 + 8, 8), 8), :] = second[0] + second[1]
        return carry

    for g, load in enumerate(loads):
        load.wait()
        lax.fori_loop(g * share, (g + 1) * share, one, 0)
    joint = jnp.concatenate(
        [
            acc[pl.ds(8 * part + j, count, stride=16), :] + acc[pl.ds(8 * part + 4 + j, count, stride=16), :]
            for part in range(2)
            for j in range(chunks)
        ],
        axis=1,
    )
    top = joint.astype(jnp.bfloat16)
    rest = (joint - top.astype(jnp.float32)).astype(jnp.bfloat16)
    both = jnp.dot(jnp.concatenate([top, rest], axis=0), high_ref[...], preferred_element_type=jnp.float32)
    out = both[:count] + both[count:] + jnp.dot(top, low_ref[...], preferred_element_type=jnp.float32)
    time_dev = main_ref.shape[1]
    main_ref[...] = out[:, :time_dev]
    early_ref[...] = out[:, time_dev:]


def detect(slots, blocks, q, forward, high, low, count, stations, freqs, time_dev):
    rows = sum(b.shape[0] for b in blocks)
    whole = pl.BlockSpec(memory_space=pltpu.VMEM)
    return pl.pallas_call(
        functools.partial(detect_kernel, len(blocks), count, stations, freqs),
        in_specs=[pl.BlockSpec(memory_space=pltpu.SMEM)] + [whole] * len(blocks)
        + [pl.BlockSpec(memory_space=pltpu.HBM)]
        + [whole] * 3,
        out_specs=[whole, whole],
        out_shape=[
            jax.ShapeDtypeStruct((count, time_dev), jnp.float32),
            jax.ShapeDtypeStruct((count, time_dev // 2), jnp.float32),
        ],
        scratch_shapes=[
            pltpu.VMEM((rows * 16, HOLD), jnp.float32),
            pltpu.VMEM((count * 16, HOLD), jnp.float32),
            pltpu.VMEM(q.shape, q.dtype),
            pltpu.SemaphoreType.DMA((GROUPS,)),
        ],
        compiler_params=pltpu.CompilerParams(vmem_limit_bytes=VMEM_K2),
        cost_estimate=pl.CostEstimate(flops=rows * time_dev * freqs * 4, bytes_accessed=count * stations * 8 * HOLD * 4, transcendentals=0),
        name="detect",
    )(slots, *blocks, pltpu.with_memory_space_constraint(q, pltpu.HBM), forward, high, low)


def route(change):
    dx, dz, dc = change
    code = (dx * 4 + dz) * 2 + dc
    return [(i, i ^ code) for i in range(32)]


def per_device(records, templates, channels, moveouts):
    per, time_dev = records.shape
    batches, count, stations, length = templates.shape
    freqs = (time_dev + EXTRA) // 2 + 1
    forward, phase, high, low = (jnp.asarray(t) for t in host_tables(time_dev))
    swap = lambda block, change: lax.ppermute(block, "tmpl", route(change))

    q, own = template_spectra(templates.reshape(-1, length), moveouts.reshape(-1, HOLD), records, forward, phase, freqs)
    line = [own] + [swap(records, (0, d, 0)) for d in (1, 2, 3)]
    line = jnp.concatenate(line, axis=0)
    plane = [line] + [swap(line, (d, 0, 0)) for d in (1, 2, 3)]
    blocks = plane + [swap(block, (0, 0, 1)) for block in plane]

    apart = (channels // per) ^ lax.axis_index("tmpl")
    place = ((apart & 1) * 16 + (apart >> 1)) * per + channels % per
    slots = (place * 16).reshape(-1, stations)

    main, early = detect(slots, blocks, q, forward, high, low, batches * count, stations, freqs, time_dev)
    earlier = lax.ppermute(early, "tm", [(i, i - 1) for i in range(1, lax.axis_size("tm"))])
    out = main + jnp.pad(earlier, ((0, 0), (time_dev - earlier.shape[1], 0)))
    return out.reshape(batches, count, time_dev)


def solution(mesh):
    placed = (
        P("tmpl", "tm"),
        P(None, "tmpl", None, None),
        P(None, "tmpl", None),
        P(None, "tmpl", None),
    )
    return jax.shard_map(
        per_device, mesh=mesh, in_specs=placed, out_specs=P(None, "tmpl", "tm"), check_vma=False
    )
```

```python
import functools
import math

import jax
import jax.numpy as jnp
import numpy as np
from jax import lax
from jax.experimental import pallas as pl
from jax.experimental.pallas import tpu as pltpu
from jax.sharding import PartitionSpec as P

L = 200
LAGS = 56
EXTRA = L + LAGS - 2
HOLD = 128
LAG_ROWS = 64
VMEM_K1 = 8 << 20
VMEM_K2 = 18 << 20


def angles(samples, freqs, width):
    return 2.0 * math.pi / width * (samples[:, None] * freqs[None, :] % width)


def host_tables(time_dev):
    width = time_dev + EXTRA
    freqs = width // 2 + 1
    freq = np.arange(freqs)
    ang = angles(np.arange(time_dev), freq, width)
    forward = np.concatenate([np.cos(ang), np.sin(ang)], axis=1).astype(np.float32).astype(jnp.bfloat16)
    turn = angles(np.arange(LAGS), freq, width)
    phase = np.zeros((2 * LAG_ROWS, 2 * freqs), jnp.bfloat16)
    phase[:LAGS], phase[LAG_ROWS : LAG_ROWS + LAGS] = halves(np.concatenate([np.cos(turn), np.sin(turn)], axis=1))
    weight = np.where((freq == 0) | (freq == freqs - 1), 1.0, 2.0) / width
    early = np.arange(time_dev // 2, time_dev) + EXTRA
    tau = np.concatenate([np.arange(time_dev), early])
    back = angles(tau, freq, width)
    inverse = np.concatenate([np.cos(back) * weight, np.sin(back) * weight], axis=1)
    inverse[time_dev:][early < time_dev] = 0.0
    return forward, phase, *halves(inverse.T)


def halves(table):
    table = table.astype(np.float32)
    high = table.astype(jnp.bfloat16)
    return high, (table - high.astype(np.float32)).astype(jnp.bfloat16)


def template_kernel(step, freqs, lag_ref, slot_ref, record_hbm, wave_hbm, forward_hbm, phase_hbm, out, own_ref, place_ref, waves, forward, phases, sems, own_sem):
    starts = range(0, wave_hbm.shape[0], step)
    loads = [pltpu.make_async_copy(forward_hbm, forward, sems.at[0]), pltpu.make_async_copy(phase_hbm, phases, sems.at[1])]
    for n, start in enumerate(starts):
        part = pl.ds(start, step)
        loads.append(pltpu.make_async_copy(wave_hbm.at[part], waves.at[part], sems.at[2 + n]))
    for load in loads:
        load.start()
    own = pltpu.make_async_copy(record_hbm, own_ref, own_sem)
    own.start()
    place_ref[...] = slot_ref[...]
    for n, start in enumerate(starts):
        for load in loads[:3] if n == 0 else loads[2 + n : 3 + n]:
            load.wait()
        lag = jnp.concatenate([lag_ref[pl.ds((start + at) // HOLD, 1), :] for at in range(0, step, HOLD)], axis=1)
        lag_row = lax.broadcasted_iota(jnp.int32, (2 * LAG_ROWS, step), 0) & (LAG_ROWS - 1)
        chosen = (lag_row == lag).astype(jnp.float32).astype(jnp.bfloat16)
        phase = lax.dot_general(chosen, phases[...], (((0,), (0,)), ((), ())), preferred_element_type=jnp.float32)
        dft = jnp.dot(waves[pl.ds(start, step), :], forward[...], preferred_element_type=jnp.float32)
        for j in range(freqs // HOLD):
            low, high = slice(j * HOLD, (j + 1) * HOLD), slice(freqs + j * HOLD, freqs + (j + 1) * HOLD)
            h_cos, h_sin, c_theta, s_theta = dft[:, low], dft[:, high], phase[:, low], phase[:, high]
            out[pl.ds(start * 8 + j, step, stride=8), :] = h_cos * c_theta - h_sin * s_theta
            out[pl.ds(start * 8 + 4 + j, step, stride=8), :] = h_cos * s_theta + h_sin * c_theta
    own.wait()


def template_spectra(waves, lags, slots, records, forward, phase, freqs):
    count, length = waves.shape
    whole = pl.BlockSpec(memory_space=pltpu.VMEM)
    step = 512
    return pl.pallas_call(
        functools.partial(template_kernel, step, freqs),
        in_specs=[whole] * 2 + [pl.BlockSpec(memory_space=pltpu.HBM)] * 4,
        out_specs=[whole] * 3,
        out_shape=[
            jax.ShapeDtypeStruct((count * 8, HOLD), jnp.float32),
            jax.ShapeDtypeStruct(records.shape, records.dtype),
            jax.ShapeDtypeStruct(slots.shape, slots.dtype),
        ],
        scratch_shapes=[
            pltpu.VMEM(waves.shape, waves.dtype),
            pltpu.VMEM((length, 2 * freqs), forward.dtype),
            pltpu.VMEM(phase.shape, phase.dtype),
            pltpu.SemaphoreType.DMA((2 + count // step,)),
            pltpu.SemaphoreType.DMA,
        ],
        compiler_params=pltpu.CompilerParams(vmem_limit_bytes=VMEM_K1),
        cost_estimate=pl.CostEstimate(flops=count * length * freqs * 4, bytes_accessed=count * 8 * HOLD * 4, transcendentals=0),
        name="template_spectra",
    )(lags, slots, *(pltpu.with_memory_space_constraint(a, pltpu.HBM) for a in (records, waves, forward[:length], phase)))


def join_kernel(*refs):
    *parts, out = refs
    at = 0
    for part in parts:
        out[pl.ds(at, part.shape[0]), :] = part[...]
        at += part.shape[0]


def join(parts):
    rows = sum(part.shape[0] for part in parts)
    whole = pl.BlockSpec(memory_space=pltpu.VMEM)
    return pl.pallas_call(
        join_kernel,
        in_specs=[whole] * len(parts),
        out_specs=whole,
        out_shape=jax.ShapeDtypeStruct((rows, parts[0].shape[1]), parts[0].dtype),
        compiler_params=pltpu.CompilerParams(vmem_limit_bytes=2 << 20),
        name="join",
    )(*parts)


def detect_kernel(n_blocks, count, stations, freqs, slot_ref, *refs):
    blocks, (q, forward_ref, high_ref, low_ref, main_ref, early_ref, table, acc) = refs[:n_blocks], refs[n_blocks:]
    chunks = freqs // HOLD
    size = blocks[0].shape[0]
    for b, block in enumerate(blocks):
        dft = jnp.dot(block[...], forward_ref[...], preferred_element_type=jnp.float32)
        for j in range(chunks):
            real = dft[:, j * HOLD : (j + 1) * HOLD]
            imag = dft[:, freqs + j * HOLD : freqs + (j + 1) * HOLD]
            start = b * size * 16
            table[pl.ds(start + j, size, stride=16), :] = real
            table[pl.ds(start + 4 + j, size, stride=16), :] = imag
            table[pl.ds(start + 8 + j, size, stride=16), :] = imag
            table[pl.ds(start + 12 + j, size, stride=16), :] = -real

    def one(t, carry):
        first = [jnp.zeros((8, HOLD), jnp.float32)] * 2
        second = list(first)
        weights = q.at[pl.ds(pl.multiple_of(t * stations * 8, stations * 8), stations * 8), :]
        for k in range(stations):
            slot = pl.multiple_of(slot_ref[t, k], 16)
            weight = weights[k * 8 : k * 8 + 8, :]
            first[k % 2] += weight * table[pl.ds(slot, 8), :]
            second[k % 2] += weight * table[pl.ds(slot + 8, 8), :]
        acc[pl.ds(pl.multiple_of(t * 16, 16), 8), :] = first[0] + first[1]
        acc[pl.ds(pl.multiple_of(t * 16 + 8, 8), 8), :] = second[0] + second[1]
        return carry

    lax.fori_loop(0, count, one, 0)
    joint = jnp.concatenate(
        [
            acc[pl.ds(8 * part + j, count, stride=16), :] + acc[pl.ds(8 * part + 4 + j, count, stride=16), :]
            for part in range(2)
            for j in range(chunks)
        ],
        axis=1,
    )
    top = joint.astype(jnp.bfloat16)
    rest = (joint - top.astype(jnp.float32)).astype(jnp.bfloat16)
    both = jnp.dot(jnp.concatenate([top, rest], axis=0), high_ref[...], preferred_element_type=jnp.float32)
    out = both[:count] + both[count:] + jnp.dot(top, low_ref[...], preferred_element_type=jnp.float32)
    time_dev = main_ref.shape[1]
    main_ref[...] = out[:, :time_dev]
    early_ref[...] = out[:, time_dev:]


def detect(slots, blocks, q, forward, high, low, count, stations, freqs, time_dev):
    rows = sum(b.shape[0] for b in blocks)
    whole = pl.BlockSpec(memory_space=pltpu.VMEM)
    return pl.pallas_call(
        functools.partial(detect_kernel, len(blocks), count, stations, freqs),
        in_specs=[pl.BlockSpec(memory_space=pltpu.SMEM)] + [whole] * (len(blocks) + 4),
        out_specs=[whole, whole],
        out_shape=[
            jax.ShapeDtypeStruct((count, time_dev), jnp.float32),
            jax.ShapeDtypeStruct((count, time_dev // 2), jnp.float32),
        ],
        scratch_shapes=[
            pltpu.VMEM((rows * 16, HOLD), jnp.float32),
            pltpu.VMEM((count * 16, HOLD), jnp.float32),
        ],
        compiler_params=pltpu.CompilerParams(vmem_limit_bytes=VMEM_K2),
        cost_estimate=pl.CostEstimate(flops=rows * time_dev * freqs * 4, bytes_accessed=count * stations * 8 * HOLD * 4, transcendentals=0),
        name="detect",
    )(slots, *blocks, q, forward, high, low)


def route(change):
    dx, dz, dc = change
    code = (dx * 4 + dz) * 2 + dc
    return [(i, i ^ code) for i in range(32)]


def per_device(records, templates, channels, moveouts):
    per, time_dev = records.shape
    batches, count, stations, length = templates.shape
    freqs = (time_dev + EXTRA) // 2 + 1
    forward, phase, high, low = (jnp.asarray(t) for t in host_tables(time_dev))
    swap = lambda block, change: lax.ppermute(block, "tmpl", route(change))

    apart = (channels // per) ^ lax.axis_index("tmpl")
    place = ((apart & 1) * 16 + (apart >> 1)) * per + channels % per
    slots = (place * 16).reshape(-1, stations)

    q, own, slots = template_spectra(
        templates.reshape(-1, length), moveouts.reshape(-1, HOLD), slots, records, forward, phase, freqs
    )
    line = join([own] + [swap(records, (0, d, 0)) for d in (1, 2, 3)])
    plane = [line] + [swap(line, (d, 0, 0)) for d in (1, 2, 3)]
    blocks = plane + [swap(block, (0, 0, 1)) for block in plane]

    main, early = detect(slots, blocks, q, forward, high, low, batches * count, stations, freqs, time_dev)
    earlier = lax.ppermute(early, "tm", [(i, i - 1) for i in range(1, lax.axis_size("tm"))])
    out = main + jnp.pad(earlier, ((0, 0), (time_dev - earlier.shape[1], 0)))
    return out.reshape(batches, count, time_dev)


def solution(mesh):
    placed = (
        P("tmpl", "tm"),
        P(None, "tmpl", None, None),
        P(None, "tmpl", None),
        P(None, "tmpl", None),
    )
    return jax.shard_map(
        per_device, mesh=mesh, in_specs=placed, out_specs=P(None, "tmpl", "tm"), check_vma=False
    )
```

```python
import functools
import math

import jax
import jax.numpy as jnp
import numpy as np
from jax import lax
from jax.experimental import pallas as pl
from jax.experimental.pallas import tpu as pltpu
from jax.sharding import PartitionSpec as P

L = 200
LAGS = 56
EXTRA = L + LAGS - 2
HOLD = 128
LAG_ROWS = 64
VMEM_K1 = 20 << 20
VMEM_K2 = 24 << 20


def angles(samples, freqs, width):
    return 2.0 * math.pi / width * (samples[:, None] * freqs[None, :] % width)


def host_tables(time_dev):
    width = time_dev + EXTRA
    freqs = width // 2 + 1
    freq = np.arange(freqs)
    ang = angles(np.arange(time_dev), freq, width)
    forward = np.concatenate([np.cos(ang), np.sin(ang)], axis=1).astype(np.float32).astype(jnp.bfloat16)
    turn = angles(np.arange(LAGS), freq, width)
    phase = np.zeros((2 * LAG_ROWS, 2 * freqs), jnp.bfloat16)
    phase[:LAGS], phase[LAG_ROWS : LAG_ROWS + LAGS] = halves(np.concatenate([np.cos(turn), np.sin(turn)], axis=1))
    weight = np.where((freq == 0) | (freq == freqs - 1), 1.0, 2.0) / width
    early = np.arange(time_dev // 2, time_dev) + EXTRA
    tau = np.concatenate([np.arange(time_dev), early])
    back = angles(tau, freq, width)
    inverse = np.concatenate([np.cos(back) * weight, np.sin(back) * weight], axis=1)
    inverse[time_dev:][early < time_dev] = 0.0
    return forward, phase, *halves(inverse.T)


def halves(table):
    table = table.astype(np.float32)
    high = table.astype(jnp.bfloat16)
    return high, (table - high.astype(np.float32)).astype(jnp.bfloat16)


def load_kernel(count, *refs):
    sources, targets, sems = refs[:count], refs[count:-1], refs[-1]
    copies = [pltpu.make_async_copy(src, dst, sems.at[n]) for n, (src, dst) in enumerate(zip(sources, targets))]
    for copy in copies:
        copy.start()
    for copy in copies:
        copy.wait()


def load(arrays):
    return pl.pallas_call(
        functools.partial(load_kernel, len(arrays)),
        in_specs=[pl.BlockSpec(memory_space=pltpu.HBM)] * len(arrays),
        out_specs=[pl.BlockSpec(memory_space=pltpu.VMEM)] * len(arrays),
        out_shape=[jax.ShapeDtypeStruct(a.shape, a.dtype) for a in arrays],
        scratch_shapes=[pltpu.SemaphoreType.DMA((len(arrays),))],
        compiler_params=pltpu.CompilerParams(vmem_limit_bytes=8 << 20),
        name="load",
    )(*(pltpu.with_memory_space_constraint(a, pltpu.HBM) for a in arrays))


def template_kernel(step, freqs, lag_ref, slot_ref, line_ref, waves, forward, phases, out, line_out, slot_out):
    line_out[...] = line_ref[...]
    slot_out[...] = slot_ref[...]
    for start in range(0, waves.shape[0], step):
        lag = jnp.concatenate([lag_ref[pl.ds((start + at) // HOLD, 1), :] for at in range(0, step, HOLD)], axis=1)
        lag_row = lax.broadcasted_iota(jnp.int32, (2 * LAG_ROWS, step), 0) & (LAG_ROWS - 1)
        chosen = (lag_row == lag).astype(jnp.float32).astype(jnp.bfloat16)
        phase = lax.dot_general(chosen, phases[...], (((0,), (0,)), ((), ())), preferred_element_type=jnp.float32)
        dft = jnp.dot(waves[pl.ds(start, step), :], forward[...], preferred_element_type=jnp.float32)
        for j in range(freqs // HOLD):
            low, high = slice(j * HOLD, (j + 1) * HOLD), slice(freqs + j * HOLD, freqs + (j + 1) * HOLD)
            h_cos, h_sin, c_theta, s_theta = dft[:, low], dft[:, high], phase[:, low], phase[:, high]
            out[pl.ds(start * 8 + j, step, stride=8), :] = h_cos * c_theta - h_sin * s_theta
            out[pl.ds(start * 8 + 4 + j, step, stride=8), :] = h_cos * s_theta + h_sin * c_theta


def template_spectra(lags, slots, line, waves, forward, phase, freqs):
    count, length = waves.shape
    whole = pl.BlockSpec(memory_space=pltpu.VMEM)
    return pl.pallas_call(
        functools.partial(template_kernel, 512, freqs),
        in_specs=[whole] * 6,
        out_specs=[whole] * 3,
        out_shape=[
            jax.ShapeDtypeStruct((count * 8, HOLD), jnp.float32),
            jax.ShapeDtypeStruct(line.shape, line.dtype),
            jax.ShapeDtypeStruct(slots.shape, slots.dtype),
        ],
        compiler_params=pltpu.CompilerParams(vmem_limit_bytes=VMEM_K1),
        cost_estimate=pl.CostEstimate(flops=count * length * freqs * 4, bytes_accessed=count * 8 * HOLD * 4, transcendentals=0),
        name="template_spectra",
    )(lags, slots, line, waves, forward, phase)


def join_kernel(*refs):
    *parts, out = refs
    at = 0
    for part in parts:
        out[pl.ds(at, part.shape[0]), :] = part[...]
        at += part.shape[0]


def join(parts):
    rows = sum(part.shape[0] for part in parts)
    whole = pl.BlockSpec(memory_space=pltpu.VMEM)
    return pl.pallas_call(
        join_kernel,
        in_specs=[whole] * len(parts),
        out_specs=whole,
        out_shape=jax.ShapeDtypeStruct((rows, parts[0].shape[1]), parts[0].dtype),
        compiler_params=pltpu.CompilerParams(vmem_limit_bytes=2 << 20),
        name="join",
    )(*parts)


def detect_kernel(n_blocks, count, stations, freqs, slot_ref, *refs):
    blocks, (q, forward_ref, high_ref, low_ref, main_ref, early_ref, table, acc) = refs[:n_blocks], refs[n_blocks:]
    chunks = freqs // HOLD
    size = blocks[0].shape[0]
    for b, block in enumerate(blocks):
        dft = jnp.dot(block[...], forward_ref[...], preferred_element_type=jnp.float32)
        for j in range(chunks):
            start = b * size * 8
            table[pl.ds(start + j, size, stride=8), :] = dft[:, j * HOLD : (j + 1) * HOLD]
            table[pl.ds(start + 4 + j, size, stride=8), :] = dft[:, freqs + j * HOLD : freqs + (j + 1) * HOLD]

    def one(t, carry):
        first = [jnp.zeros((8, HOLD), jnp.float32)] * 2
        second = list(first)
        weights = q.at[pl.ds(pl.multiple_of(t * stations * 8, stations * 8), stations * 8), :]
        for k in range(stations):
            record = table[pl.ds(pl.multiple_of(slot_ref[t, k], 8), 8), :]
            weight = weights[k * 8 : k * 8 + 8, :]
            first[k % 2] += weight * record
            second[k % 2] += weight * pltpu.roll(record, 4, 0)
        acc[pl.ds(pl.multiple_of(t * 16, 16), 8), :] = first[0] + first[1]
        acc[pl.ds(pl.multiple_of(t * 16 + 8, 8), 8), :] = second[0] + second[1]
        return carry

    lax.fori_loop(0, count, one, 0)
    joint = jnp.concatenate(
        [acc[pl.ds(j, count, stride=16), :] + acc[pl.ds(4 + j, count, stride=16), :] for j in range(chunks)]
        + [acc[pl.ds(8 + j, count, stride=16), :] - acc[pl.ds(12 + j, count, stride=16), :] for j in range(chunks)],
        axis=1,
    )
    top = joint.astype(jnp.bfloat16)
    rest = (joint - top.astype(jnp.float32)).astype(jnp.bfloat16)
    both = jnp.dot(jnp.concatenate([top, rest], axis=0), high_ref[...], preferred_element_type=jnp.float32)
    out = both[:count] + both[count:] + jnp.dot(top, low_ref[...], preferred_element_type=jnp.float32)
    time_dev = main_ref.shape[1]
    main_ref[...] = out[:, :time_dev]
    early_ref[...] = out[:, time_dev:]


def detect(slots, blocks, q, forward, high, low, count, stations, freqs, time_dev):
    rows = sum(b.shape[0] for b in blocks)
    whole = pl.BlockSpec(memory_space=pltpu.VMEM)
    return pl.pallas_call(
        functools.partial(detect_kernel, len(blocks), count, stations, freqs),
        in_specs=[pl.BlockSpec(memory_space=pltpu.SMEM)] + [whole] * (len(blocks) + 4),
        out_specs=[whole, whole],
        out_shape=[
            jax.ShapeDtypeStruct((count, time_dev), jnp.float32),
            jax.ShapeDtypeStruct((count, time_dev // 2), jnp.float32),
        ],
        scratch_shapes=[
            pltpu.VMEM((rows * 8, HOLD), jnp.float32),
            pltpu.VMEM((count * 16, HOLD), jnp.float32),
        ],
        compiler_params=pltpu.CompilerParams(vmem_limit_bytes=VMEM_K2),
        cost_estimate=pl.CostEstimate(flops=rows * time_dev * freqs * 4, bytes_accessed=count * stations * 8 * HOLD * 4, transcendentals=0),
        name="detect",
    )(slots, *blocks, q, forward, high, low)


def route(change):
    dx, dz, dc = change
    code = (dx * 4 + dz) * 2 + dc
    return [(i, i ^ code) for i in range(32)]


def per_device(records, templates, channels, moveouts):
    per, time_dev = records.shape
    batches, count, stations, length = templates.shape
    freqs = (time_dev + EXTRA) // 2 + 1
    forward, phase, high, low = (jnp.asarray(t) for t in host_tables(time_dev))
    swap = lambda block, change: lax.ppermute(block, "tmpl", route(change))

    apart = (channels // per) ^ lax.axis_index("tmpl")
    place = ((apart & 1) * 16 + (apart >> 1)) * per + channels % per
    slots = (place * 8).reshape(-1, stations)

    own, waves, head, phase = load([records, templates.reshape(-1, length), forward[:length], phase])
    line = join([own] + [swap(records, (0, d, 0)) for d in (1, 2, 3)])
    plane = [swap(line, (d, 0, 0)) for d in (1, 2, 3)]
    q, line_q, slots = template_spectra(moveouts.reshape(-1, HOLD), slots, line, waves, head, phase, freqs)
    blocks = [line] + plane + [swap(block, (0, 0, 1)) for block in [line_q] + plane]

    main, early = detect(slots, blocks, q, forward, high, low, batches * count, stations, freqs, time_dev)
    earlier = lax.ppermute(early, "tm", [(i, i - 1) for i in range(1, lax.axis_size("tm"))])
    out = main + jnp.pad(earlier, ((0, 0), (time_dev - earlier.shape[1], 0)))
    return out.reshape(batches, count, time_dev)


def solution(mesh):
    placed = (
        P("tmpl", "tm"),
        P(None, "tmpl", None, None),
        P(None, "tmpl", None),
        P(None, "tmpl", None),
    )
    return jax.shard_map(
        per_device, mesh=mesh, in_specs=placed, out_specs=P(None, "tmpl", "tm"), check_vma=False
    )
```

```python
import functools
import math

import jax
import jax.numpy as jnp
import numpy as np
from jax import lax
from jax.experimental import pallas as pl
from jax.experimental.pallas import tpu as pltpu
from jax.sharding import PartitionSpec as P

L = 200
LAGS = 56
EXTRA = L + LAGS - 2
HOLD = 128
LAG_ROWS = 64
Z_ORDER = (3, 2, 1)
X_ORDER = (3, 1, 2)
VMEM_K1 = 20 << 20
VMEM_K2 = 24 << 20
VMEM_D1 = 10 << 20


def angles(samples, freqs, width):
    return 2.0 * math.pi / width * (samples[:, None] * freqs[None, :] % width)


def host_tables(time_dev):
    width = time_dev + EXTRA
    freqs = width // 2 + 1
    freq = np.arange(freqs)
    ang = angles(np.arange(time_dev), freq, width)
    forward = np.concatenate([np.cos(ang), np.sin(ang)], axis=1).astype(np.float32).astype(jnp.bfloat16)
    turn = angles(np.arange(LAGS), freq, width)
    phase = np.zeros((2 * LAG_ROWS, 2 * freqs), jnp.bfloat16)
    phase[:LAGS], phase[LAG_ROWS : LAG_ROWS + LAGS] = halves(np.concatenate([np.cos(turn), np.sin(turn)], axis=1))
    weight = np.where((freq == 0) | (freq == freqs - 1), 1.0, 2.0) / width
    early = np.arange(time_dev // 2, time_dev) + EXTRA
    tau = np.concatenate([np.arange(time_dev), early])
    back = angles(tau, freq, width)
    inverse = np.concatenate([np.cos(back) * weight, np.sin(back) * weight], axis=1)
    inverse[time_dev:][early < time_dev] = 0.0
    return forward, phase, *halves(inverse.T)


def halves(table):
    table = table.astype(np.float32)
    high = table.astype(jnp.bfloat16)
    return high, (table - high.astype(np.float32)).astype(jnp.bfloat16)


def load_kernel(count, *refs):
    sources, targets, sems = refs[:count], refs[count:-1], refs[-1]
    copies = [pltpu.make_async_copy(src, dst, sems.at[n]) for n, (src, dst) in enumerate(zip(sources, targets))]
    for copy in copies:
        copy.start()
    for copy in copies:
        copy.wait()


def load(arrays):
    return pl.pallas_call(
        functools.partial(load_kernel, len(arrays)),
        in_specs=[pl.BlockSpec(memory_space=pltpu.HBM)] * len(arrays),
        out_specs=[pl.BlockSpec(memory_space=pltpu.VMEM)] * len(arrays),
        out_shape=[jax.ShapeDtypeStruct(a.shape, a.dtype) for a in arrays],
        scratch_shapes=[pltpu.SemaphoreType.DMA((len(arrays),))],
        compiler_params=pltpu.CompilerParams(vmem_limit_bytes=8 << 20),
        name="load",
    )(*(pltpu.with_memory_space_constraint(a, pltpu.HBM) for a in arrays))


def template_kernel(step, freqs, lag_ref, slot_ref, line_ref, waves, forward, phases, out, line_out, slot_out):
    line_out[...] = line_ref[...]
    slot_out[...] = slot_ref[...]
    for start in range(0, waves.shape[0], step):
        lag = jnp.concatenate([lag_ref[pl.ds((start + at) // HOLD, 1), :] for at in range(0, step, HOLD)], axis=1)
        lag_row = lax.broadcasted_iota(jnp.int32, (2 * LAG_ROWS, step), 0) & (LAG_ROWS - 1)
        chosen = (lag_row == lag).astype(jnp.float32).astype(jnp.bfloat16)
        phase = lax.dot_general(chosen, phases[...], (((0,), (0,)), ((), ())), preferred_element_type=jnp.float32)
        dft = jnp.dot(waves[pl.ds(start, step), :], forward[...], preferred_element_type=jnp.float32)
        for j in range(freqs // HOLD):
            low, high = slice(j * HOLD, (j + 1) * HOLD), slice(freqs + j * HOLD, freqs + (j + 1) * HOLD)
            h_cos, h_sin, c_theta, s_theta = dft[:, low], dft[:, high], phase[:, low], phase[:, high]
            out[pl.ds(start * 8 + j, step, stride=8), :] = h_cos * c_theta - h_sin * s_theta
            out[pl.ds(start * 8 + 4 + j, step, stride=8), :] = h_cos * s_theta + h_sin * c_theta


def template_spectra(lags, slots, line, waves, forward, phase, freqs):
    count, length = waves.shape
    whole = pl.BlockSpec(memory_space=pltpu.VMEM)
    return pl.pallas_call(
        functools.partial(template_kernel, 512, freqs),
        in_specs=[whole] * 6,
        out_specs=[whole] * 3,
        out_shape=[
            jax.ShapeDtypeStruct((count * 8, HOLD), jnp.float32),
            jax.ShapeDtypeStruct(line.shape, line.dtype),
            jax.ShapeDtypeStruct(slots.shape, slots.dtype),
        ],
        compiler_params=pltpu.CompilerParams(vmem_limit_bytes=VMEM_K1),
        cost_estimate=pl.CostEstimate(flops=count * length * freqs * 4, bytes_accessed=count * 8 * HOLD * 4, transcendentals=0),
        name="template_spectra",
    )(lags, slots, line, waves, forward, phase)


def join_kernel(*refs):
    *parts, out = refs
    at = 0
    for part in parts:
        out[pl.ds(at, part.shape[0]), :] = part[...]
        at += part.shape[0]


def join(parts):
    rows = sum(part.shape[0] for part in parts)
    whole = pl.BlockSpec(memory_space=pltpu.VMEM)
    return pl.pallas_call(
        join_kernel,
        in_specs=[whole] * len(parts),
        out_specs=whole,
        out_shape=jax.ShapeDtypeStruct((rows, parts[0].shape[1]), parts[0].dtype),
        compiler_params=pltpu.CompilerParams(vmem_limit_bytes=2 << 20),
        name="join",
    )(*parts)


def fill_table(blocks, forward_ref, table, first, freqs):
    for b, block in enumerate(blocks):
        size = block.shape[0]
        dft = jnp.dot(block[...], forward_ref[...], preferred_element_type=jnp.float32)
        for j in range(freqs // HOLD):
            start = (first + b * size) * 8 + j
            table[pl.ds(start, size, stride=8), :] = dft[:, j * HOLD : (j + 1) * HOLD]
            table[pl.ds(start + 4, size, stride=8), :] = dft[:, freqs + j * HOLD : freqs + (j + 1) * HOLD]


def record_kernel(freqs, *refs):
    *blocks, forward_ref, table = refs
    fill_table(blocks, forward_ref, table, 0, freqs)


def record_spectra(blocks, forward, freqs, parts):
    rows = sum(b.shape[0] for b in blocks)
    whole = pl.BlockSpec(memory_space=pltpu.VMEM)
    return pl.pallas_call(
        functools.partial(record_kernel, freqs),
        in_specs=[whole] * (len(blocks) + 1),
        out_specs=whole,
        out_shape=jax.ShapeDtypeStruct((parts * rows * 8, HOLD), jnp.float32),
        compiler_params=pltpu.CompilerParams(vmem_limit_bytes=VMEM_D1),
        cost_estimate=pl.CostEstimate(flops=rows * forward.shape[0] * freqs * 4, bytes_accessed=rows * 8 * HOLD * 4, transcendentals=0),
        name="record_spectra",
    )(*blocks, forward)


def detect_kernel(n_blocks, count, stations, freqs, slot_ref, *refs):
    blocks, (_, q, forward_ref, high_ref, low_ref, main_ref, early_ref, table, acc) = refs[:n_blocks], refs[n_blocks:]
    chunks = freqs // HOLD
    fill_table(blocks, forward_ref, table, table.shape[0] // 16, freqs)

    def one(t, carry):
        first = [jnp.zeros((8, HOLD), jnp.float32)] * 2
        second = list(first)
        weights = q.at[pl.ds(pl.multiple_of(t * stations * 8, stations * 8), stations * 8), :]
        for k in range(stations):
            record = table[pl.ds(pl.multiple_of(slot_ref[t, k], 8), 8), :]
            weight = weights[k * 8 : k * 8 + 8, :]
            first[k % 2] += weight * record
            second[k % 2] += weight * pltpu.roll(record, 4, 0)
        acc[pl.ds(pl.multiple_of(t * 16, 16), 8), :] = first[0] + first[1]
        acc[pl.ds(pl.multiple_of(t * 16 + 8, 8), 8), :] = second[0] + second[1]
        return carry

    lax.fori_loop(0, count, one, 0, unroll=2)
    joint = jnp.concatenate(
        [acc[pl.ds(j, count, stride=16), :] + acc[pl.ds(4 + j, count, stride=16), :] for j in range(chunks)]
        + [acc[pl.ds(8 + j, count, stride=16), :] - acc[pl.ds(12 + j, count, stride=16), :] for j in range(chunks)],
        axis=1,
    )
    top = joint.astype(jnp.bfloat16)
    rest = (joint - top.astype(jnp.float32)).astype(jnp.bfloat16)
    both = jnp.dot(jnp.concatenate([top, rest], axis=0), high_ref[...], preferred_element_type=jnp.float32)
    out = both[:count] + both[count:] + jnp.dot(top, low_ref[...], preferred_element_type=jnp.float32)
    time_dev = main_ref.shape[1]
    main_ref[...] = out[:, :time_dev]
    early_ref[...] = out[:, time_dev:].astype(early_ref.dtype)


def detect(slots, blocks, table, q, forward, high, low, count, stations, freqs, time_dev):
    rows = sum(b.shape[0] for b in blocks)
    whole = pl.BlockSpec(memory_space=pltpu.VMEM)
    return pl.pallas_call(
        functools.partial(detect_kernel, len(blocks), count, stations, freqs),
        in_specs=[pl.BlockSpec(memory_space=pltpu.SMEM)] + [whole] * (len(blocks) + 5),
        out_specs=[whole] * 3,
        out_shape=[
            jax.ShapeDtypeStruct((count, time_dev), jnp.float32),
            jax.ShapeDtypeStruct((count, time_dev // 2), jnp.bfloat16),
            jax.ShapeDtypeStruct(table.shape, table.dtype),
        ],
        input_output_aliases={1 + len(blocks): 2},
        scratch_shapes=[
            pltpu.VMEM((count * 16, HOLD), jnp.float32),
        ],
        compiler_params=pltpu.CompilerParams(vmem_limit_bytes=VMEM_K2),
        cost_estimate=pl.CostEstimate(flops=rows * time_dev * freqs * 4, bytes_accessed=count * stations * 8 * HOLD * 4, transcendentals=0),
        name="detect",
    )(slots, *blocks, table, q, forward, high, low)[:2]


def route(change):
    dx, dz, dc = change
    code = (dx * 4 + dz) * 2 + dc
    return [(i, i ^ code) for i in range(32)]


def position_bits(order):
    return sum((1 + n) << (2 * d) for n, d in enumerate(order))


def per_device(records, templates, channels, moveouts):
    per, time_dev = records.shape
    batches, count, stations, length = templates.shape
    freqs = (time_dev + EXTRA) // 2 + 1
    forward, phase, high, low = (jnp.asarray(t) for t in host_tables(time_dev))
    swap = lambda block, change: lax.ppermute(block, "tmpl", route(change))

    apart = (channels // per) ^ lax.axis_index("tmpl")
    rank_z = (position_bits(Z_ORDER) >> (apart & 6)) & 3
    rank_x = (position_bits(X_ORDER) >> ((apart >> 2) & 6)) & 3
    place = ((apart & 1) * 16 + rank_x * 4 + rank_z) * per + channels % per
    slots = (place * 8).reshape(-1, stations)

    own, waves, head, phase = load([records, templates.reshape(-1, length), forward[:length], phase])
    line = join([own] + [swap(records, (0, d, 0)) for d in Z_ORDER])
    plane = [swap(line, (d, 0, 0)) for d in X_ORDER]
    q, line_q, slots = template_spectra(moveouts.reshape(-1, HOLD), slots, line, waves, head, phase, freqs)
    near = [line] + plane
    far = [swap(block, (0, 0, 1)) for block in [line_q] + plane]
    table = record_spectra(near, forward, freqs, 2)

    main, early = detect(slots, far, table, q, forward, high, low, batches * count, stations, freqs, time_dev)
    earlier = lax.ppermute(early, "tm", [(i, i - 1) for i in range(1, lax.axis_size("tm"))])
    earlier = earlier.astype(jnp.float32)
    out = main + jnp.pad(earlier, ((0, 0), (time_dev - earlier.shape[1], 0)))
    return out.reshape(batches, count, time_dev)


def solution(mesh):
    placed = (
        P("tmpl", "tm"),
        P(None, "tmpl", None, None),
        P(None, "tmpl", None),
        P(None, "tmpl", None),
    )
    return jax.shard_map(
        per_device, mesh=mesh, in_specs=placed, out_specs=P(None, "tmpl", "tm"), check_vma=False
    )
```

```python
import functools
import math

import jax
import jax.numpy as jnp
import numpy as np
from jax import lax
from jax.experimental import pallas as pl
from jax.experimental.pallas import tpu as pltpu
from jax.sharding import PartitionSpec as P

L = 200
LAGS = 56
EXTRA = L + LAGS - 2
HOLD = 128
LAG_ROWS = 64
Z_ORDER = (3, 2, 1)
X_ORDER = (2, 1, 3)
VMEM_K1 = 12 << 20
VMEM_K2 = 12 << 20
VMEM_D1 = 4 << 20


def angles(samples, freqs, width):
    return 2.0 * math.pi / width * (samples[:, None] * freqs[None, :] % width)


def host_tables(time_dev):
    width = time_dev + EXTRA
    freqs = width // 2 + 1
    freq = np.arange(freqs)
    ang = angles(np.arange(time_dev), freq, width)
    forward = np.concatenate([np.cos(ang), np.sin(ang)], axis=1).astype(np.float32).astype(jnp.bfloat16)
    turn = angles(np.arange(LAGS), freq, width)
    phase = np.zeros((2 * LAG_ROWS, 2 * freqs), jnp.bfloat16)
    phase[:LAGS], phase[LAG_ROWS : LAG_ROWS + LAGS] = halves(np.concatenate([np.cos(turn), np.sin(turn)], axis=1))
    weight = np.where((freq == 0) | (freq == freqs - 1), 1.0, 2.0) / width
    early = np.arange(time_dev // 2, time_dev) + EXTRA
    tau = np.concatenate([np.arange(time_dev), early])
    back = angles(tau, freq, width)
    inverse = np.concatenate([np.cos(back) * weight, np.sin(back) * weight], axis=1)
    inverse[time_dev:][early < time_dev] = 0.0
    return forward, phase, *halves(inverse.T)


def halves(table):
    table = table.astype(np.float32)
    high = table.astype(jnp.bfloat16)
    return high, (table - high.astype(np.float32)).astype(jnp.bfloat16)


def load_kernel(count, *refs):
    sources, targets, sems = refs[:count], refs[count:-1], refs[-1]
    copies = [pltpu.make_async_copy(src, dst, sems.at[n]) for n, (src, dst) in enumerate(zip(sources, targets))]
    for copy in copies:
        copy.start()
    for copy in copies:
        copy.wait()


def load(arrays):
    return pl.pallas_call(
        functools.partial(load_kernel, len(arrays)),
        in_specs=[pl.BlockSpec(memory_space=pltpu.HBM)] * len(arrays),
        out_specs=[pl.BlockSpec(memory_space=pltpu.VMEM)] * len(arrays),
        out_shape=[jax.ShapeDtypeStruct(a.shape, a.dtype) for a in arrays],
        scratch_shapes=[pltpu.SemaphoreType.DMA((len(arrays),))],
        compiler_params=pltpu.CompilerParams(vmem_limit_bytes=8 << 20),
        name="load",
    )(*(pltpu.with_memory_space_constraint(a, pltpu.HBM) for a in arrays))


def template_kernel(step, freqs, lag_ref, line_ref, waves, head, forward, phases, out, line_out, table):
    line_out[...] = line_ref[...]
    for start in range(0, waves.shape[0], step):
        lag = jnp.concatenate([lag_ref[pl.ds((start + at) // HOLD, 1), :] for at in range(0, step, HOLD)], axis=1)
        lag_row = lax.broadcasted_iota(jnp.int32, (2 * LAG_ROWS, step), 0) & (LAG_ROWS - 1)
        chosen = (lag_row == lag).astype(jnp.float32).astype(jnp.bfloat16)
        phase = lax.dot_general(chosen, phases[...], (((0,), (0,)), ((), ())), preferred_element_type=jnp.float32)
        dft = jnp.dot(waves[pl.ds(start, step), :], head[...], preferred_element_type=jnp.float32)
        for j in range(freqs // HOLD):
            low, high = slice(j * HOLD, (j + 1) * HOLD), slice(freqs + j * HOLD, freqs + (j + 1) * HOLD)
            h_cos, h_sin, c_theta, s_theta = dft[:, low], dft[:, high], phase[:, low], phase[:, high]
            out[pl.ds(start * 8 + j, step, stride=8), :] = h_cos * c_theta - h_sin * s_theta
            out[pl.ds(start * 8 + 4 + j, step, stride=8), :] = h_cos * s_theta + h_sin * c_theta
    fill_table([line_ref], forward, table, 0, freqs)


def template_spectra(lags, line, waves, head, forward, phase, rows, freqs):
    count, length = waves.shape
    whole = pl.BlockSpec(memory_space=pltpu.VMEM)
    return pl.pallas_call(
        functools.partial(template_kernel, 512, freqs),
        in_specs=[whole] * 6,
        out_specs=[whole] * 3,
        out_shape=[
            jax.ShapeDtypeStruct((count * 8, HOLD), jnp.float32),
            jax.ShapeDtypeStruct(line.shape, line.dtype),
            jax.ShapeDtypeStruct((rows * 8, HOLD), jnp.float32),
        ],
        compiler_params=pltpu.CompilerParams(vmem_limit_bytes=VMEM_K1),
        cost_estimate=pl.CostEstimate(flops=count * length * freqs * 4, bytes_accessed=count * 8 * HOLD * 4, transcendentals=0),
        name="template_spectra",
    )(lags, line, waves, head, forward, phase)


def join_kernel(*refs):
    *parts, out = refs
    at = 0
    for part in parts:
        out[pl.ds(at, part.shape[0]), :] = part[...]
        at += part.shape[0]


def join(parts):
    rows = sum(part.shape[0] for part in parts)
    whole = pl.BlockSpec(memory_space=pltpu.VMEM)
    return pl.pallas_call(
        join_kernel,
        in_specs=[whole] * len(parts),
        out_specs=whole,
        out_shape=jax.ShapeDtypeStruct((rows, parts[0].shape[1]), parts[0].dtype),
        compiler_params=pltpu.CompilerParams(vmem_limit_bytes=2 << 20),
        name="join",
    )(*parts)


def fill_table(blocks, forward_ref, table, first, freqs):
    for b, block in enumerate(blocks):
        size = block.shape[0]
        dft = jnp.dot(block[...], forward_ref[...], preferred_element_type=jnp.float32)
        for j in range(freqs // HOLD):
            start = (first + b * size) * 8 + j
            table[pl.ds(start, size, stride=8), :] = dft[:, j * HOLD : (j + 1) * HOLD]
            table[pl.ds(start + 4, size, stride=8), :] = dft[:, freqs + j * HOLD : freqs + (j + 1) * HOLD]


def record_kernel(freqs, first, *refs):
    *blocks, forward_ref, _, table = refs
    fill_table(blocks, forward_ref, table, first, freqs)


def record_spectra(blocks, forward, table, first, freqs):
    rows = sum(b.shape[0] for b in blocks)
    whole = pl.BlockSpec(memory_space=pltpu.VMEM)
    return pl.pallas_call(
        functools.partial(record_kernel, freqs, first),
        in_specs=[whole] * (len(blocks) + 2),
        out_specs=whole,
        out_shape=jax.ShapeDtypeStruct(table.shape, table.dtype),
        input_output_aliases={len(blocks) + 1: 0},
        compiler_params=pltpu.CompilerParams(vmem_limit_bytes=VMEM_D1),
        cost_estimate=pl.CostEstimate(flops=rows * forward.shape[0] * freqs * 4, bytes_accessed=rows * 8 * HOLD * 4, transcendentals=0),
        name="record_spectra",
    )(*blocks, forward, table)


def inverse(parts, high, low):
    count = parts.shape[0] // 2
    both = jnp.dot(parts, high, preferred_element_type=jnp.float32)
    return both[:count] + both[count:] + jnp.dot(parts[:count], low, preferred_element_type=jnp.float32)


def inverse_kernel(parts_ref, high_ref, low_ref, main_ref):
    columns = slice(0, main_ref.shape[1])
    main_ref[...] = inverse(parts_ref[...], high_ref[:, columns], low_ref[:, columns])


def own_window(parts, high, low, time_dev):
    whole = pl.BlockSpec(memory_space=pltpu.VMEM)
    count = parts.shape[0] // 2
    return pl.pallas_call(
        inverse_kernel,
        in_specs=[whole] * 3,
        out_specs=whole,
        out_shape=jax.ShapeDtypeStruct((count, time_dev), jnp.float32),
        compiler_params=pltpu.CompilerParams(vmem_limit_bytes=VMEM_D1),
        cost_estimate=pl.CostEstimate(flops=6 * count * parts.shape[1] * time_dev, bytes_accessed=1 << 22, transcendentals=0),
        name="own_window",
    )(parts, high, low)


def detect_kernel(n_blocks, count, stations, freqs, slots, *refs):
    blocks, (_, q, forward_ref, high_ref, low_ref, parts_ref, early_ref, table, acc, slot_ref, sem) = refs[:n_blocks], refs[n_blocks:]
    load = pltpu.make_async_copy(slots, slot_ref, sem)
    load.start()
    chunks = freqs // HOLD
    fill_table(blocks, forward_ref, table, table.shape[0] // 16, freqs)
    load.wait()

    def one(t, carry):
        first = [jnp.zeros((8, HOLD), jnp.float32)] * 2
        second = list(first)
        weights = q.at[pl.ds(pl.multiple_of(t * stations * 8, stations * 8), stations * 8), :]
        for k in range(stations):
            record = table[pl.ds(pl.multiple_of(slot_ref[t, k], 8), 8), :]
            weight = weights[k * 8 : k * 8 + 8, :]
            first[k % 2] += weight * record
            second[k % 2] += weight * pltpu.roll(record, 4, 0)
        acc[pl.ds(pl.multiple_of(t * 16, 16), 8), :] = first[0] + first[1]
        acc[pl.ds(pl.multiple_of(t * 16 + 8, 8), 8), :] = second[0] + second[1]
        return carry

    lax.fori_loop(0, count, one, 0, unroll=2)
    joint = jnp.concatenate(
        [acc[pl.ds(j, count, stride=16), :] + acc[pl.ds(4 + j, count, stride=16), :] for j in range(chunks)]
        + [acc[pl.ds(8 + j, count, stride=16), :] - acc[pl.ds(12 + j, count, stride=16), :] for j in range(chunks)],
        axis=1,
    )
    top = joint.astype(jnp.bfloat16)
    rest = (joint - top.astype(jnp.float32)).astype(jnp.bfloat16)
    parts_ref[:count, :] = top
    parts_ref[count:, :] = rest
    columns = slice(high_ref.shape[1] - early_ref.shape[1], None)
    early_ref[...] = inverse(parts_ref[...], high_ref[:, columns], low_ref[:, columns]).astype(early_ref.dtype)


def detect(slots, blocks, table, q, forward, high, low, count, stations, freqs, time_dev):
    rows = sum(b.shape[0] for b in blocks)
    whole = pl.BlockSpec(memory_space=pltpu.VMEM)
    return pl.pallas_call(
        functools.partial(detect_kernel, len(blocks), count, stations, freqs),
        in_specs=[whole] * (len(blocks) + 6),
        out_specs=[whole] * 3,
        out_shape=[
            jax.ShapeDtypeStruct((2 * count, 2 * freqs), jnp.bfloat16),
            jax.ShapeDtypeStruct((count, time_dev // 2), jnp.bfloat16),
            jax.ShapeDtypeStruct(table.shape, table.dtype),
        ],
        input_output_aliases={1 + len(blocks): 2},
        scratch_shapes=[
            pltpu.VMEM((count * 16, HOLD), jnp.float32),
            pltpu.SMEM(slots.shape, slots.dtype),
            pltpu.SemaphoreType.DMA,
        ],
        compiler_params=pltpu.CompilerParams(vmem_limit_bytes=VMEM_K2),
        cost_estimate=pl.CostEstimate(flops=rows * time_dev * freqs * 4, bytes_accessed=count * stations * 8 * HOLD * 4, transcendentals=0),
        name="detect",
    )(slots, *blocks, table, q, forward, high, low)[:2]


def route(change):
    dx, dz, dc = change
    code = (dx * 4 + dz) * 2 + dc
    return [(i, i ^ code) for i in range(32)]


def position_bits(order):
    return sum((1 + n) << (2 * d) for n, d in enumerate(order))


def per_device(records, templates, channels, moveouts):
    per, time_dev = records.shape
    batches, count, stations, length = templates.shape
    freqs = (time_dev + EXTRA) // 2 + 1
    forward, phase, high, low = (jnp.asarray(t) for t in host_tables(time_dev))
    swap = lambda block, change: lax.ppermute(block, "tmpl", route(change))

    apart = (channels // per) ^ lax.axis_index("tmpl")
    rank_z = (position_bits(Z_ORDER) >> (apart & 6)) & 3
    rank_x = (position_bits(X_ORDER) >> ((apart >> 2) & 6)) & 3
    place = ((apart & 1) * 16 + rank_x * 4 + rank_z) * per + channels % per
    slots = (place * 8).reshape(-1, stations)

    waves, lags = templates.reshape(-1, length), moveouts.reshape(-1, HOLD)
    own, waves, head, forward, phase, lags, slots, high, low = load(
        [records, waves, forward[:length], forward, phase, lags, slots, high, low]
    )
    line = join([own] + [swap(records, (0, d, 0)) for d in Z_ORDER])
    plane = [swap(line, (d, 0, 0)) for d in X_ORDER]
    q, line_q, table = template_spectra(lags, line, waves, head, forward, phase, 32 * per, freqs)
    far = [swap(block, (0, 0, 1)) for block in [line_q] + plane]
    table = record_spectra(plane, forward, table, line.shape[0], freqs)
    parts, early = detect(slots, far, table, q, forward, high, low, batches * count, stations, freqs, time_dev)
    main = own_window(parts, high, low, time_dev)
    earlier = lax.ppermute(early, "tm", [(i, i - 1) for i in range(1, lax.axis_size("tm"))])
    earlier = earlier.astype(jnp.float32)
    out = main + jnp.pad(earlier, ((0, 0), (time_dev - earlier.shape[1], 0)))
    return out.reshape(batches, count, time_dev)


def solution(mesh):
    placed = (
        P("tmpl", "tm"),
        P(None, "tmpl", None, None),
        P(None, "tmpl", None),
        P(None, "tmpl", None),
    )
    return jax.shard_map(
        per_device, mesh=mesh, in_specs=placed, out_specs=P(None, "tmpl", "tm"), check_vma=False
    )
```

```python
import functools
import math

import jax
import jax.numpy as jnp
import numpy as np
from jax import lax
from jax.experimental import pallas as pl
from jax.experimental.pallas import tpu as pltpu
from jax.sharding import PartitionSpec as P

L = 200
LAGS = 56
EXTRA = L + LAGS - 2
HOLD = 128
LAG_ROWS = 64
SPREAD_ROWS = 64
Z_ORDER = (3, 2, 1)
X_ORDER = (2, 1, 3)
VMEM_K1 = 12 << 20
VMEM_K2 = 12 << 20
VMEM_D1 = 4 << 20


def angles(samples, freqs, width):
    return 2.0 * math.pi / width * (samples[:, None] * freqs[None, :] % width)


def host_tables(time_dev):
    width = time_dev + EXTRA
    freqs = width // 2 + 1
    freq = np.arange(freqs)
    ang = angles(np.arange(time_dev), freq, width)
    forward = np.concatenate([np.cos(ang), np.sin(ang)], axis=1).astype(np.float32).astype(jnp.bfloat16)
    turn = angles(np.arange(LAGS), freq, width)
    phase = np.zeros((2 * LAG_ROWS, 2 * freqs), jnp.bfloat16)
    phase[:LAGS], phase[LAG_ROWS : LAG_ROWS + LAGS] = halves(np.concatenate([np.cos(turn), np.sin(turn)], axis=1))
    weight = np.where((freq == 0) | (freq == freqs - 1), 1.0, 2.0) / width
    early = np.arange(time_dev // 2, time_dev) + EXTRA
    tau = np.concatenate([np.arange(time_dev), early])
    back = angles(tau, freq, width)
    inverse = np.concatenate([np.cos(back) * weight, np.sin(back) * weight], axis=1)
    inverse[time_dev:][early < time_dev] = 0.0
    return forward, phase, *halves(inverse.T)


def halves(table):
    table = table.astype(np.float32)
    high = table.astype(jnp.bfloat16)
    return high, (table - high.astype(np.float32)).astype(jnp.bfloat16)


def load_kernel(count, per, *refs):
    sources, (*targets, slot_ref, channel_ref, sems) = refs[:count], refs[count:]
    targets = [channel_ref, *targets]
    copies = [pltpu.make_async_copy(src, dst, sems.at[n]) for n, (src, dst) in enumerate(zip(sources, targets))]
    for copy in copies:
        copy.start()
    copies[0].wait()
    channel = channel_ref[...]
    owner = (channel * reciprocal(per)) >> 16
    apart = owner ^ lax.axis_index("tmpl")
    rank_z = (position_bits(Z_ORDER) >> (apart & 6)) & 3
    rank_x = (position_bits(X_ORDER) >> ((apart >> 2) & 6)) & 3
    slot_ref[...] = (((apart & 1) * 16 + rank_x * 4 + rank_z) * per + channel - owner * per) * 8
    for copy in copies[1:]:
        copy.wait()


def reciprocal(per):
    m = (1 << 16) // per + 1
    n = np.arange(32 * per)
    assert (n * m >> 16 == n // per).all()
    return m


def load(arrays, channels, per):
    whole = pl.BlockSpec(memory_space=pltpu.VMEM)
    return pl.pallas_call(
        functools.partial(load_kernel, len(arrays) + 1, per),
        in_specs=[pl.BlockSpec(memory_space=pltpu.HBM)] * (len(arrays) + 1),
        out_specs=[whole] * (len(arrays) + 1),
        out_shape=[jax.ShapeDtypeStruct(a.shape, a.dtype) for a in (*arrays, channels)],
        scratch_shapes=[pltpu.VMEM(channels.shape, channels.dtype), pltpu.SemaphoreType.DMA((len(arrays) + 1,))],
        compiler_params=pltpu.CompilerParams(vmem_limit_bytes=12 << 20),
        name="load",
    )(*(pltpu.with_memory_space_constraint(a, pltpu.HBM) for a in (channels, *arrays)))


def spread_table(stations):
    at = np.arange(8 * stations)
    spread = np.zeros((SPREAD_ROWS + 16, 8 * stations), jnp.bfloat16)
    spread[at % stations, at] = 1
    spread[SPREAD_ROWS + at // stations, at] = 1
    return spread


def template_kernel(step, freqs, lag_ref, spread_ref, line_ref, waves, head, forward, phases, out, line_out, table):
    line_out[...] = line_ref[...]
    stations = lag_ref.shape[1]
    lags = lag_ref[...].astype(jnp.float32).astype(jnp.bfloat16)
    lags = jnp.dot(lags, spread_ref[:stations, :], preferred_element_type=jnp.float32)
    stretch = spread_ref[pl.ds(SPREAD_ROWS, 8), :].astype(jnp.float32)
    lag_row = (lax.broadcasted_iota(jnp.int32, (2 * LAG_ROWS, step), 0) & (LAG_ROWS - 1)).astype(jnp.float32)
    for start in range(0, waves.shape[0], step):
        group = start // stations
        lag = jnp.sum(lags[group : group + 8] * stretch, axis=0, keepdims=True)
        chosen = (lag_row == lag).astype(jnp.float32).astype(jnp.bfloat16)
        phase = lax.dot_general(chosen, phases[...], (((0,), (0,)), ((), ())), preferred_element_type=jnp.float32)
        dft = jnp.dot(waves[pl.ds(start, step), :], head[...], preferred_element_type=jnp.float32)
        for j in range(freqs // HOLD):
            low, high = slice(j * HOLD, (j + 1) * HOLD), slice(freqs + j * HOLD, freqs + (j + 1) * HOLD)
            h_cos, h_sin, c_theta, s_theta = dft[:, low], dft[:, high], phase[:, low], phase[:, high]
            out[pl.ds(start * 8 + j, step, stride=8), :] = h_cos * c_theta - h_sin * s_theta
            out[pl.ds(start * 8 + 4 + j, step, stride=8), :] = h_cos * s_theta + h_sin * c_theta
    fill_table([line_ref], forward, table, 0, freqs)


def template_spectra(lags, spread, line, waves, head, forward, phase, rows, freqs):
    count, length = waves.shape
    whole = pl.BlockSpec(memory_space=pltpu.VMEM)
    return pl.pallas_call(
        functools.partial(template_kernel, 8 * lags.shape[1], freqs),
        in_specs=[whole] * 7,
        out_specs=[whole] * 3,
        out_shape=[
            jax.ShapeDtypeStruct((count * 8, HOLD), jnp.float32),
            jax.ShapeDtypeStruct(line.shape, line.dtype),
            jax.ShapeDtypeStruct((rows * 8, HOLD), jnp.float32),
        ],
        compiler_params=pltpu.CompilerParams(vmem_limit_bytes=VMEM_K1),
        cost_estimate=pl.CostEstimate(flops=count * length * freqs * 4, bytes_accessed=count * 8 * HOLD * 4, transcendentals=0),
        name="template_spectra",
    )(lags, spread, line, waves, head, forward, phase)


def join_kernel(*refs):
    *parts, out = refs
    at = 0
    for part in parts:
        out[pl.ds(at, part.shape[0]), :] = part[...]
        at += part.shape[0]


def join(parts):
    rows = sum(part.shape[0] for part in parts)
    whole = pl.BlockSpec(memory_space=pltpu.VMEM)
    return pl.pallas_call(
        join_kernel,
        in_specs=[whole] * len(parts),
        out_specs=whole,
        out_shape=jax.ShapeDtypeStruct((rows, parts[0].shape[1]), parts[0].dtype),
        compiler_params=pltpu.CompilerParams(vmem_limit_bytes=2 << 20),
        name="join",
    )(*parts)


def fill_table(blocks, forward_ref, table, first, freqs):
    for b, block in enumerate(blocks):
        size = block.shape[0]
        dft = jnp.dot(block[...], forward_ref[...], preferred_element_type=jnp.float32)
        for j in range(freqs // HOLD):
            start = (first + b * size) * 8 + j
            table[pl.ds(start, size, stride=8), :] = dft[:, j * HOLD : (j + 1) * HOLD]
            table[pl.ds(start + 4, size, stride=8), :] = dft[:, freqs + j * HOLD : freqs + (j + 1) * HOLD]


def record_kernel(freqs, first, *refs):
    *blocks, forward_ref, _, table = refs
    fill_table(blocks, forward_ref, table, first, freqs)


def record_spectra(blocks, forward, table, first, freqs):
    rows = sum(b.shape[0] for b in blocks)
    whole = pl.BlockSpec(memory_space=pltpu.VMEM)
    return pl.pallas_call(
        functools.partial(record_kernel, freqs, first),
        in_specs=[whole] * (len(blocks) + 2),
        out_specs=whole,
        out_shape=jax.ShapeDtypeStruct(table.shape, table.dtype),
        input_output_aliases={len(blocks) + 1: 0},
        compiler_params=pltpu.CompilerParams(vmem_limit_bytes=VMEM_D1),
        cost_estimate=pl.CostEstimate(flops=rows * forward.shape[0] * freqs * 4, bytes_accessed=rows * 8 * HOLD * 4, transcendentals=0),
        name="record_spectra",
    )(*blocks, forward, table)


def inverse(parts, high, low):
    count = parts.shape[0] // 2
    both = jnp.dot(parts, high, preferred_element_type=jnp.float32)
    return both[:count] + both[count:] + jnp.dot(parts[:count], low, preferred_element_type=jnp.float32)


def inverse_kernel(parts_ref, high_ref, low_ref, main_ref):
    columns = slice(0, main_ref.shape[1])
    main_ref[...] = inverse(parts_ref[...], high_ref[:, columns], low_ref[:, columns])


def own_window(parts, high, low, time_dev):
    whole = pl.BlockSpec(memory_space=pltpu.VMEM)
    count = parts.shape[0] // 2
    return pl.pallas_call(
        inverse_kernel,
        in_specs=[whole] * 3,
        out_specs=whole,
        out_shape=jax.ShapeDtypeStruct((count, time_dev), jnp.float32),
        compiler_params=pltpu.CompilerParams(vmem_limit_bytes=VMEM_D1),
        cost_estimate=pl.CostEstimate(flops=6 * count * parts.shape[1] * time_dev, bytes_accessed=1 << 22, transcendentals=0),
        name="own_window",
    )(parts, high, low)


def detect_kernel(n_blocks, count, stations, freqs, slots, *refs):
    blocks, (_, q, forward_ref, high_ref, low_ref, parts_ref, early_ref, table, acc, slot_ref, sem) = refs[:n_blocks], refs[n_blocks:]
    load = pltpu.make_async_copy(slots, slot_ref, sem)
    load.start()
    chunks = freqs // HOLD
    fill_table(blocks, forward_ref, table, table.shape[0] // 16, freqs)
    load.wait()

    def one(t, carry):
        first = [jnp.zeros((8, HOLD), jnp.float32)] * 2
        second = list(first)
        weights = q.at[pl.ds(pl.multiple_of(t * stations * 8, stations * 8), stations * 8), :]
        for k in range(stations):
            record = table[pl.ds(pl.multiple_of(slot_ref[t, k], 8), 8), :]
            weight = weights[k * 8 : k * 8 + 8, :]
            first[k % 2] += weight * record
            second[k % 2] += weight * pltpu.roll(record, 4, 0)
        acc[pl.ds(pl.multiple_of(t * 16, 16), 8), :] = first[0] + first[1]
        acc[pl.ds(pl.multiple_of(t * 16 + 8, 8), 8), :] = second[0] + second[1]
        return carry

    lax.fori_loop(0, count, one, 0, unroll=2)
    joint = jnp.concatenate(
        [acc[pl.ds(j, count, stride=16), :] + acc[pl.ds(4 + j, count, stride=16), :] for j in range(chunks)]
        + [acc[pl.ds(8 + j, count, stride=16), :] - acc[pl.ds(12 + j, count, stride=16), :] for j in range(chunks)],
        axis=1,
    )
    top = joint.astype(jnp.bfloat16)
    rest = (joint - top.astype(jnp.float32)).astype(jnp.bfloat16)
    parts_ref[:count, :] = top
    parts_ref[count:, :] = rest
    columns = slice(high_ref.shape[1] - early_ref.shape[1], None)
    early_ref[...] = inverse(parts_ref[...], high_ref[:, columns], low_ref[:, columns]).astype(early_ref.dtype)


def detect(slots, blocks, table, q, forward, high, low, count, stations, freqs, time_dev):
    rows = sum(b.shape[0] for b in blocks)
    whole = pl.BlockSpec(memory_space=pltpu.VMEM)
    return pl.pallas_call(
        functools.partial(detect_kernel, len(blocks), count, stations, freqs),
        in_specs=[whole] * (len(blocks) + 6),
        out_specs=[whole] * 3,
        out_shape=[
            jax.ShapeDtypeStruct((2 * count, 2 * freqs), jnp.bfloat16),
            jax.ShapeDtypeStruct((count, time_dev // 2), jnp.bfloat16),
            jax.ShapeDtypeStruct(table.shape, table.dtype),
        ],
        input_output_aliases={1 + len(blocks): 2},
        scratch_shapes=[
            pltpu.VMEM((count * 16, HOLD), jnp.float32),
            pltpu.SMEM(slots.shape, slots.dtype),
            pltpu.SemaphoreType.DMA,
        ],
        compiler_params=pltpu.CompilerParams(vmem_limit_bytes=VMEM_K2),
        cost_estimate=pl.CostEstimate(flops=rows * time_dev * freqs * 4, bytes_accessed=count * stations * 8 * HOLD * 4, transcendentals=0),
        name="detect",
    )(slots, *blocks, table, q, forward, high, low)[:2]


def route(change):
    dx, dz, dc = change
    code = (dx * 4 + dz) * 2 + dc
    return [(i, i ^ code) for i in range(32)]


def position_bits(order):
    return sum((1 + n) << (2 * d) for n, d in enumerate(order))


def per_device(records, templates, channels, moveouts):
    per, time_dev = records.shape
    batches, count, stations, length = templates.shape
    freqs = (time_dev + EXTRA) // 2 + 1
    forward, phase, high, low = (jnp.asarray(t) for t in host_tables(time_dev))
    swap = lambda block, change: lax.ppermute(block, "tmpl", route(change))

    spread = jnp.asarray(spread_table(stations))
    own, waves, head, forward, phase, lags, spread, high, low, slots = load(
        [
            records,
            templates.reshape(-1, length),
            forward[:length],
            forward,
            phase,
            moveouts.reshape(-1, stations),
            spread,
            high,
            low,
        ],
        channels.reshape(-1, stations),
        per,
    )
    line = join([own] + [swap(records, (0, d, 0)) for d in Z_ORDER])
    plane = [swap(line, (d, 0, 0)) for d in X_ORDER]
    q, line_q, table = template_spectra(lags, spread, line, waves, head, forward, phase, 32 * per, freqs)
    far = [swap(block, (0, 0, 1)) for block in [line_q] + plane]
    table = record_spectra(plane, forward, table, line.shape[0], freqs)
    parts, early = detect(slots, far, table, q, forward, high, low, batches * count, stations, freqs, time_dev)
    main = own_window(parts, high, low, time_dev)
    earlier = lax.ppermute(early, "tm", [(i, i - 1) for i in range(1, lax.axis_size("tm"))])
    earlier = earlier.astype(jnp.float32)
    out = main + jnp.pad(earlier, ((0, 0), (time_dev - earlier.shape[1], 0)))
    return out.reshape(batches, count, time_dev)


def solution(mesh):
    placed = (
        P("tmpl", "tm"),
        P(None, "tmpl", None, None),
        P(None, "tmpl", None),
        P(None, "tmpl", None),
    )
    return jax.shard_map(
        per_device, mesh=mesh, in_specs=placed, out_specs=P(None, "tmpl", "tm"), check_vma=False
    )
```

```python
import functools
import math

import jax
import jax.numpy as jnp
import numpy as np
from jax import lax
from jax.experimental import pallas as pl
from jax.experimental.pallas import tpu as pltpu
from jax.sharding import PartitionSpec as P

L = 200
LAGS = 56
EXTRA = L + LAGS - 2
HOLD = 128
LAG_ROWS = 64
SPREAD_ROWS = 64
Z_ORDER = (3, 1, 2)
X_ORDER = (2, 1, 3)
VMEM_K1 = 12 << 20
VMEM_K2 = 12 << 20
VMEM_D1 = 4 << 20


def angles(samples, freqs, width):
    return 2.0 * math.pi / width * (samples[:, None] * freqs[None, :] % width)


def host_tables(time_dev):
    width = time_dev + EXTRA
    freqs = width // 2 + 1
    freq = np.arange(freqs)
    ang = angles(np.arange(time_dev), freq, width)
    forward = np.concatenate([np.cos(ang), np.sin(ang)], axis=1).astype(np.float32).astype(jnp.bfloat16)
    turn = angles(np.arange(LAGS), freq, width)
    phase = np.zeros((2 * LAG_ROWS, 2 * freqs), jnp.bfloat16)
    phase[:LAGS], phase[LAG_ROWS : LAG_ROWS + LAGS] = halves(np.concatenate([np.cos(turn), np.sin(turn)], axis=1))
    weight = np.where((freq == 0) | (freq == freqs - 1), 1.0, 2.0) / width
    early = np.arange(time_dev // 2, time_dev) + EXTRA
    tau = np.concatenate([np.arange(time_dev), early])
    back = angles(tau, freq, width)
    inverse = np.concatenate([np.cos(back) * weight, np.sin(back) * weight], axis=1)
    inverse[time_dev:][early < time_dev] = 0.0
    return forward, phase, *halves(inverse.T)


def halves(table):
    table = table.astype(np.float32)
    high = table.astype(jnp.bfloat16)
    return high, (table - high.astype(np.float32)).astype(jnp.bfloat16)


def load_kernel(count, per, *refs):
    sources, (*targets, slot_ref, channel_ref, sems) = refs[:count], refs[count:]
    targets = [channel_ref, *targets]
    copies = [pltpu.make_async_copy(src, dst, sems.at[n]) for n, (src, dst) in enumerate(zip(sources, targets))]
    for copy in copies:
        copy.start()
    copies[0].wait()
    channel = channel_ref[...]
    owner = (channel * reciprocal(per)) >> 16
    apart = owner ^ lax.axis_index("tmpl")
    rank_z = (position_bits(Z_ORDER) >> (apart & 6)) & 3
    rank_x = (position_bits(X_ORDER) >> ((apart >> 2) & 6)) & 3
    slot_ref[...] = (((apart & 1) * 16 + rank_x * 4 + rank_z) * per + channel - owner * per) * 8
    for copy in copies[1:]:
        copy.wait()


def reciprocal(per):
    m = (1 << 16) // per + 1
    n = np.arange(32 * per)
    assert (n * m >> 16 == n // per).all()
    return m


def load(arrays, channels, per):
    whole = pl.BlockSpec(memory_space=pltpu.VMEM)
    return pl.pallas_call(
        functools.partial(load_kernel, len(arrays) + 1, per),
        in_specs=[pl.BlockSpec(memory_space=pltpu.HBM)] * (len(arrays) + 1),
        out_specs=[whole] * (len(arrays) + 1),
        out_shape=[jax.ShapeDtypeStruct(a.shape, a.dtype) for a in (*arrays, channels)],
        scratch_shapes=[pltpu.VMEM(channels.shape, channels.dtype), pltpu.SemaphoreType.DMA((len(arrays) + 1,))],
        compiler_params=pltpu.CompilerParams(vmem_limit_bytes=12 << 20),
        name="load",
    )(*(pltpu.with_memory_space_constraint(a, pltpu.HBM) for a in (channels, *arrays)))


def spread_table(stations):
    at = np.arange(8 * stations)
    spread = np.zeros((SPREAD_ROWS + 16, 8 * stations), jnp.bfloat16)
    spread[at % stations, at] = 1
    spread[SPREAD_ROWS + at // stations, at] = 1
    return spread


def template_kernel(step, freqs, lag_ref, spread_ref, line_ref, waves, head, forward, phases, out, line_out, table):
    line_out[...] = line_ref[...]
    stations = lag_ref.shape[1]
    lags = lag_ref[...].astype(jnp.float32).astype(jnp.bfloat16)
    lags = jnp.dot(lags, spread_ref[:stations, :], preferred_element_type=jnp.float32)
    stretch = spread_ref[pl.ds(SPREAD_ROWS, 8), :].astype(jnp.float32)
    lag_row = (lax.broadcasted_iota(jnp.int32, (2 * LAG_ROWS, step), 0) & (LAG_ROWS - 1)).astype(jnp.float32)
    for start in range(0, waves.shape[0], step):
        group = start // stations
        lag = jnp.sum(lags[group : group + 8] * stretch, axis=0, keepdims=True)
        chosen = (lag_row == lag).astype(jnp.float32).astype(jnp.bfloat16)
        phase = lax.dot_general(chosen, phases[...], (((0,), (0,)), ((), ())), preferred_element_type=jnp.float32)
        dft = jnp.dot(waves[pl.ds(start, step), :], head[...], preferred_element_type=jnp.float32)
        for j in range(freqs // HOLD):
            low, high = slice(j * HOLD, (j + 1) * HOLD), slice(freqs + j * HOLD, freqs + (j + 1) * HOLD)
            h_cos, h_sin, c_theta, s_theta = dft[:, low], dft[:, high], phase[:, low], phase[:, high]
            out[pl.ds(start * 8 + j, step, stride=8), :] = h_cos * c_theta - h_sin * s_theta
            out[pl.ds(start * 8 + 4 + j, step, stride=8), :] = h_cos * s_theta + h_sin * c_theta
    fill_table([line_ref], forward, table, 0, freqs)


def template_spectra(lags, spread, line, waves, head, forward, phase, rows, freqs):
    count, length = waves.shape
    whole = pl.BlockSpec(memory_space=pltpu.VMEM)
    return pl.pallas_call(
        functools.partial(template_kernel, 8 * lags.shape[1], freqs),
        in_specs=[whole] * 7,
        out_specs=[whole] * 3,
        out_shape=[
            jax.ShapeDtypeStruct((count * 8, HOLD), jnp.float32),
            jax.ShapeDtypeStruct(line.shape, line.dtype),
            jax.ShapeDtypeStruct((rows * 8, HOLD), jnp.float32),
        ],
        compiler_params=pltpu.CompilerParams(vmem_limit_bytes=VMEM_K1),
        cost_estimate=pl.CostEstimate(flops=count * length * freqs * 4, bytes_accessed=count * 8 * HOLD * 4, transcendentals=0),
        name="template_spectra",
    )(lags, spread, line, waves, head, forward, phase)


def join_kernel(*refs):
    *parts, out = refs
    at = 0
    for part in parts:
        out[pl.ds(at, part.shape[0]), :] = part[...]
        at += part.shape[0]


def join(parts):
    rows = sum(part.shape[0] for part in parts)
    whole = pl.BlockSpec(memory_space=pltpu.VMEM)
    return pl.pallas_call(
        join_kernel,
        in_specs=[whole] * len(parts),
        out_specs=whole,
        out_shape=jax.ShapeDtypeStruct((rows, parts[0].shape[1]), parts[0].dtype),
        compiler_params=pltpu.CompilerParams(vmem_limit_bytes=2 << 20),
        name="join",
    )(*parts)


def fill_table(blocks, forward_ref, table, first, freqs):
    for b, block in enumerate(blocks):
        size = block.shape[0]
        dft = jnp.dot(block[...], forward_ref[...], preferred_element_type=jnp.float32)
        for j in range(freqs // HOLD):
            start = (first + b * size) * 8 + j
            table[pl.ds(start, size, stride=8), :] = dft[:, j * HOLD : (j + 1) * HOLD]
            table[pl.ds(start + 4, size, stride=8), :] = dft[:, freqs + j * HOLD : freqs + (j + 1) * HOLD]


def record_kernel(freqs, first, *refs):
    *blocks, forward_ref, _, table = refs
    fill_table(blocks, forward_ref, table, first, freqs)


def record_spectra(blocks, forward, table, first, freqs):
    rows = sum(b.shape[0] for b in blocks)
    whole = pl.BlockSpec(memory_space=pltpu.VMEM)
    return pl.pallas_call(
        functools.partial(record_kernel, freqs, first),
        in_specs=[whole] * (len(blocks) + 2),
        out_specs=whole,
        out_shape=jax.ShapeDtypeStruct(table.shape, table.dtype),
        input_output_aliases={len(blocks) + 1: 0},
        compiler_params=pltpu.CompilerParams(vmem_limit_bytes=VMEM_D1),
        cost_estimate=pl.CostEstimate(flops=rows * forward.shape[0] * freqs * 4, bytes_accessed=rows * 8 * HOLD * 4, transcendentals=0),
        name="record_spectra",
    )(*blocks, forward, table)


def inverse(parts, high, low):
    count = parts.shape[0] // 2
    both = jnp.dot(parts, high, preferred_element_type=jnp.float32)
    return both[:count] + both[count:] + jnp.dot(parts[:count], low, preferred_element_type=jnp.float32)


def inverse_kernel(parts_ref, high_ref, low_ref, main_ref):
    columns = slice(0, main_ref.shape[1])
    main_ref[...] = inverse(parts_ref[...], high_ref[:, columns], low_ref[:, columns])


def own_window(parts, high, low, time_dev):
    whole = pl.BlockSpec(memory_space=pltpu.VMEM)
    count = parts.shape[0] // 2
    return pl.pallas_call(
        inverse_kernel,
        in_specs=[whole] * 3,
        out_specs=whole,
        out_shape=jax.ShapeDtypeStruct((count, time_dev), jnp.float32),
        compiler_params=pltpu.CompilerParams(vmem_limit_bytes=VMEM_D1),
        cost_estimate=pl.CostEstimate(flops=6 * count * parts.shape[1] * time_dev, bytes_accessed=1 << 22, transcendentals=0),
        name="own_window",
    )(parts, high, low)


def detect_kernel(n_blocks, count, stations, freqs, slots, *refs):
    blocks, (_, q, forward_ref, high_ref, low_ref, parts_ref, early_ref, table, acc, slot_ref, sem) = refs[:n_blocks], refs[n_blocks:]
    load = pltpu.make_async_copy(slots, slot_ref, sem)
    load.start()
    chunks = freqs // HOLD
    fill_table(blocks, forward_ref, table, table.shape[0] // 16, freqs)
    load.wait()

    def one(t, carry):
        first = [jnp.zeros((8, HOLD), jnp.float32)] * 2
        second = list(first)
        weights = q.at[pl.ds(pl.multiple_of(t * stations * 8, stations * 8), stations * 8), :]
        for k in range(stations):
            record = table[pl.ds(pl.multiple_of(slot_ref[t, k], 8), 8), :]
            weight = weights[k * 8 : k * 8 + 8, :]
            first[k % 2] += weight * record
            second[k % 2] += weight * pltpu.roll(record, 4, 0)
        acc[pl.ds(pl.multiple_of(t * 16, 16), 8), :] = first[0] + first[1]
        acc[pl.ds(pl.multiple_of(t * 16 + 8, 8), 8), :] = second[0] + second[1]
        return carry

    lax.fori_loop(0, count, one, 0, unroll=2)
    joint = jnp.concatenate(
        [acc[pl.ds(j, count, stride=16), :] + acc[pl.ds(4 + j, count, stride=16), :] for j in range(chunks)]
        + [acc[pl.ds(8 + j, count, stride=16), :] - acc[pl.ds(12 + j, count, stride=16), :] for j in range(chunks)],
        axis=1,
    )
    top = joint.astype(jnp.bfloat16)
    rest = (joint - top.astype(jnp.float32)).astype(jnp.bfloat16)
    parts_ref[:count, :] = top
    parts_ref[count:, :] = rest
    columns = slice(high_ref.shape[1] - early_ref.shape[1], None)
    early_ref[...] = inverse(parts_ref[...], high_ref[:, columns], low_ref[:, columns]).astype(early_ref.dtype)


def detect(slots, blocks, table, q, forward, high, low, count, stations, freqs, time_dev):
    rows = sum(b.shape[0] for b in blocks)
    whole = pl.BlockSpec(memory_space=pltpu.VMEM)
    return pl.pallas_call(
        functools.partial(detect_kernel, len(blocks), count, stations, freqs),
        in_specs=[whole] * (len(blocks) + 6),
        out_specs=[whole] * 3,
        out_shape=[
            jax.ShapeDtypeStruct((2 * count, 2 * freqs), jnp.bfloat16),
            jax.ShapeDtypeStruct((count, time_dev // 2), jnp.bfloat16),
            jax.ShapeDtypeStruct(table.shape, table.dtype),
        ],
        input_output_aliases={1 + len(blocks): 2},
        scratch_shapes=[
            pltpu.VMEM((count * 16, HOLD), jnp.float32),
            pltpu.SMEM(slots.shape, slots.dtype),
            pltpu.SemaphoreType.DMA,
        ],
        compiler_params=pltpu.CompilerParams(vmem_limit_bytes=VMEM_K2),
        cost_estimate=pl.CostEstimate(flops=rows * time_dev * freqs * 4, bytes_accessed=count * stations * 8 * HOLD * 4, transcendentals=0),
        name="detect",
    )(slots, *blocks, table, q, forward, high, low)[:2]


def route(change):
    dx, dz, dc = change
    code = (dx * 4 + dz) * 2 + dc
    return [(i, i ^ code) for i in range(32)]


def position_bits(order):
    return sum((1 + n) << (2 * d) for n, d in enumerate(order))


def per_device(records, templates, channels, moveouts):
    per, time_dev = records.shape
    batches, count, stations, length = templates.shape
    freqs = (time_dev + EXTRA) // 2 + 1
    forward, phase, high, low = (jnp.asarray(t) for t in host_tables(time_dev))
    swap = lambda block, change: lax.ppermute(block, "tmpl", route(change))

    spread = jnp.asarray(spread_table(stations))
    own, waves, head, forward, phase, lags, spread, high, low, slots = load(
        [
            records,
            templates.reshape(-1, length),
            forward[:length],
            forward,
            phase,
            moveouts.reshape(-1, stations),
            spread,
            high,
            low,
        ],
        channels.reshape(-1, stations),
        per,
    )
    line = join([own] + [swap(records, (0, d, 0)) for d in Z_ORDER])
    plane = [swap(line, (d, 0, 0)) for d in X_ORDER]
    q, line_q, table = template_spectra(lags, spread, line, waves, head, forward, phase, 32 * per, freqs)
    far = [swap(block, (0, 0, 1)) for block in [line_q] + plane]
    table = record_spectra(plane, forward, table, line.shape[0], freqs)
    parts, early = detect(slots, far, table, q, forward, high, low, batches * count, stations, freqs, time_dev)
    main = own_window(parts, high, low, time_dev)
    earlier = lax.ppermute(early, "tm", [(i, i - 1) for i in range(1, lax.axis_size("tm"))])
    earlier = earlier.astype(jnp.float32)
    out = main + jnp.pad(earlier, ((0, 0), (time_dev - earlier.shape[1], 0)))
    return out.reshape(batches, count, time_dev)


def solution(mesh):
    placed = (
        P("tmpl", "tm"),
        P(None, "tmpl", None, None),
        P(None, "tmpl", None),
        P(None, "tmpl", None),
    )
    return jax.shard_map(
        per_device, mesh=mesh, in_specs=placed, out_specs=P(None, "tmpl", "tm"), check_vma=False
    )
```

```python
import functools
import math

import jax
import jax.numpy as jnp
import numpy as np
from jax import lax
from jax.experimental import pallas as pl
from jax.experimental.pallas import tpu as pltpu
from jax.sharding import PartitionSpec as P

L = 200
LAGS = 56
EXTRA = L + LAGS - 2
HOLD = 128
LAG_ROWS = 64
SPREAD_ROWS = 64
Z_ORDER = (3, 1, 2)
X_ORDER = (2, 1, 3)
VMEM_K1 = 12 << 20
VMEM_K2 = 12 << 20
VMEM_D1 = 4 << 20


def angles(samples, freqs, width):
    return 2.0 * math.pi / width * (samples[:, None] * freqs[None, :] % width)


def host_tables(time_dev):
    width = time_dev + EXTRA
    freqs = width // 2 + 1
    freq = np.arange(freqs)
    ang = angles(np.arange(time_dev), freq, width)
    forward = np.concatenate([np.cos(ang), np.sin(ang)], axis=1).astype(np.float32).astype(jnp.bfloat16)
    turn = angles(np.arange(LAGS), freq, width)
    phase = np.zeros((2 * LAG_ROWS, 2 * freqs), jnp.bfloat16)
    phase[:LAGS], phase[LAG_ROWS : LAG_ROWS + LAGS] = halves(np.concatenate([np.cos(turn), np.sin(turn)], axis=1))
    weight = np.where((freq == 0) | (freq == freqs - 1), 1.0, 2.0) / width
    early = np.arange(time_dev // 2, time_dev) + EXTRA
    tau = np.concatenate([np.arange(time_dev), early])
    back = angles(tau, freq, width)
    inverse = np.concatenate([np.cos(back) * weight, np.sin(back) * weight], axis=1)
    inverse[time_dev:][early < time_dev] = 0.0
    return forward, phase, *halves(inverse.T)


def halves(table):
    table = table.astype(np.float32)
    high = table.astype(jnp.bfloat16)
    return high, (table - high.astype(np.float32)).astype(jnp.bfloat16)


def load_kernel(count, per, *refs):
    sources, (*targets, slot_ref, channel_ref, sems) = refs[:count], refs[count:]
    targets = [channel_ref, *targets]
    copies = [pltpu.make_async_copy(src, dst, sems.at[n]) for n, (src, dst) in enumerate(zip(sources, targets))]
    for copy in copies:
        copy.start()
    copies[0].wait()
    channel = channel_ref[...]
    owner = (channel * reciprocal(per)) >> 16
    apart = owner ^ lax.axis_index("tmpl")
    rank_z = (position_bits(Z_ORDER) >> (apart & 6)) & 3
    rank_x = (position_bits(X_ORDER) >> ((apart >> 2) & 6)) & 3
    slot_ref[...] = (((apart & 1) * 16 + rank_x * 4 + rank_z) * per + channel - owner * per) * 8
    for copy in copies[1:]:
        copy.wait()


def reciprocal(per):
    m = (1 << 16) // per + 1
    n = np.arange(32 * per)
    assert (n * m >> 16 == n // per).all()
    return m


def load(arrays, channels, per):
    whole = pl.BlockSpec(memory_space=pltpu.VMEM)
    return pl.pallas_call(
        functools.partial(load_kernel, len(arrays) + 1, per),
        in_specs=[pl.BlockSpec(memory_space=pltpu.HBM)] * (len(arrays) + 1),
        out_specs=[whole] * (len(arrays) + 1),
        out_shape=[jax.ShapeDtypeStruct(a.shape, a.dtype) for a in (*arrays, channels)],
        scratch_shapes=[pltpu.VMEM(channels.shape, channels.dtype), pltpu.SemaphoreType.DMA((len(arrays) + 1,))],
        compiler_params=pltpu.CompilerParams(vmem_limit_bytes=12 << 20),
        name="load",
    )(*(pltpu.with_memory_space_constraint(a, pltpu.HBM) for a in (channels, *arrays)))


def spread_table(stations):
    at = np.arange(8 * stations)
    spread = np.zeros((SPREAD_ROWS + 16, 8 * stations), jnp.bfloat16)
    spread[at % stations, at] = 1
    spread[SPREAD_ROWS + at // stations, at] = 1
    return spread


def template_kernel(step, freqs, lag_ref, spread_ref, line_ref, waves, head, forward, phases, out, line_out, table):
    line_out[...] = line_ref[...]
    stations = lag_ref.shape[1]
    lags = lag_ref[...].astype(jnp.float32).astype(jnp.bfloat16)
    lags = jnp.dot(lags, spread_ref[:stations, :], preferred_element_type=jnp.float32)
    stretch = spread_ref[pl.ds(SPREAD_ROWS, 8), :].astype(jnp.float32)
    lag_row = (lax.broadcasted_iota(jnp.int32, (2 * LAG_ROWS, step), 0) & (LAG_ROWS - 1)).astype(jnp.float32)
    for start in range(0, waves.shape[0], step):
        group = start // stations
        lag = jnp.sum(lags[group : group + 8] * stretch, axis=0, keepdims=True)
        chosen = (lag_row == lag).astype(jnp.float32).astype(jnp.bfloat16)
        phase = lax.dot_general(chosen, phases[...], (((0,), (0,)), ((), ())), preferred_element_type=jnp.float32)
        dft = jnp.dot(waves[pl.ds(start, step), :], head[...], preferred_element_type=jnp.float32)
        for j in range(freqs // HOLD):
            low, high = slice(j * HOLD, (j + 1) * HOLD), slice(freqs + j * HOLD, freqs + (j + 1) * HOLD)
            h_cos, h_sin, c_theta, s_theta = dft[:, low], dft[:, high], phase[:, low], phase[:, high]
            out[pl.ds(start * 8 + j, step, stride=8), :] = h_cos * c_theta - h_sin * s_theta
            out[pl.ds(start * 8 + 4 + j, step, stride=8), :] = h_cos * s_theta + h_sin * c_theta
    fill_table([line_ref], forward, table, 0, freqs)


def template_spectra(lags, spread, line, waves, head, forward, phase, rows, freqs):
    count, length = waves.shape
    whole = pl.BlockSpec(memory_space=pltpu.VMEM)
    return pl.pallas_call(
        functools.partial(template_kernel, 8 * lags.shape[1], freqs),
        in_specs=[whole] * 7,
        out_specs=[whole] * 3,
        out_shape=[
            jax.ShapeDtypeStruct((count * 8, HOLD), jnp.float32),
            jax.ShapeDtypeStruct(line.shape, line.dtype),
            jax.ShapeDtypeStruct((rows * 8, HOLD), jnp.float32),
        ],
        compiler_params=pltpu.CompilerParams(vmem_limit_bytes=VMEM_K1),
        cost_estimate=pl.CostEstimate(flops=count * length * freqs * 4, bytes_accessed=count * 8 * HOLD * 4, transcendentals=0),
        name="template_spectra",
    )(lags, spread, line, waves, head, forward, phase)


def join_kernel(*refs):
    *parts, out = refs
    at = 0
    for part in parts:
        out[pl.ds(at, part.shape[0]), :] = part[...]
        at += part.shape[0]


def join(parts):
    rows = sum(part.shape[0] for part in parts)
    whole = pl.BlockSpec(memory_space=pltpu.VMEM)
    return pl.pallas_call(
        join_kernel,
        in_specs=[whole] * len(parts),
        out_specs=whole,
        out_shape=jax.ShapeDtypeStruct((rows, parts[0].shape[1]), parts[0].dtype),
        compiler_params=pltpu.CompilerParams(vmem_limit_bytes=2 << 20),
        name="join",
    )(*parts)


def fill_table(blocks, forward_ref, table, first, freqs):
    for b, block in enumerate(blocks):
        size = block.shape[0]
        dft = jnp.dot(block[...], forward_ref[...], preferred_element_type=jnp.float32)
        for j in range(freqs // HOLD):
            start = (first + b * size) * 8 + j
            table[pl.ds(start, size, stride=8), :] = dft[:, j * HOLD : (j + 1) * HOLD]
            table[pl.ds(start + 4, size, stride=8), :] = dft[:, freqs + j * HOLD : freqs + (j + 1) * HOLD]


def record_kernel(freqs, first, *refs):
    *blocks, far_line, forward_ref, _, table = refs
    fill_table(blocks, forward_ref, table, first, freqs)
    fill_table([far_line], forward_ref, table, table.shape[0] // 16, freqs)


def record_spectra(blocks, forward, table, first, freqs):
    rows = sum(b.shape[0] for b in blocks)
    whole = pl.BlockSpec(memory_space=pltpu.VMEM)
    return pl.pallas_call(
        functools.partial(record_kernel, freqs, first),
        in_specs=[whole] * (len(blocks) + 2),
        out_specs=whole,
        out_shape=jax.ShapeDtypeStruct(table.shape, table.dtype),
        input_output_aliases={len(blocks) + 1: 0},
        compiler_params=pltpu.CompilerParams(vmem_limit_bytes=VMEM_D1),
        cost_estimate=pl.CostEstimate(flops=rows * forward.shape[0] * freqs * 4, bytes_accessed=rows * 8 * HOLD * 4, transcendentals=0),
        name="record_spectra",
    )(*blocks, forward, table)


def inverse(parts, high, low):
    count = parts.shape[0] // 2
    both = jnp.dot(parts, high, preferred_element_type=jnp.float32)
    return both[:count] + both[count:] + jnp.dot(parts[:count], low, preferred_element_type=jnp.float32)


def inverse_kernel(parts_ref, high_ref, low_ref, main_ref):
    columns = slice(0, main_ref.shape[1])
    main_ref[...] = inverse(parts_ref[...], high_ref[:, columns], low_ref[:, columns])


def own_window(parts, high, low, time_dev):
    whole = pl.BlockSpec(memory_space=pltpu.VMEM)
    count = parts.shape[0] // 2
    return pl.pallas_call(
        inverse_kernel,
        in_specs=[whole] * 3,
        out_specs=whole,
        out_shape=jax.ShapeDtypeStruct((count, time_dev), jnp.float32),
        compiler_params=pltpu.CompilerParams(vmem_limit_bytes=VMEM_D1),
        cost_estimate=pl.CostEstimate(flops=6 * count * parts.shape[1] * time_dev, bytes_accessed=1 << 22, transcendentals=0),
        name="own_window",
    )(parts, high, low)


def detect_kernel(n_blocks, count, stations, freqs, slots, *refs):
    blocks, (_, q, forward_ref, high_ref, low_ref, parts_ref, early_ref, table, acc, slot_ref, sem) = refs[:n_blocks], refs[n_blocks:]
    load = pltpu.make_async_copy(slots, slot_ref, sem)
    load.start()
    chunks = freqs // HOLD
    fill_table(blocks, forward_ref, table, table.shape[0] // 8 - n_blocks * blocks[0].shape[0], freqs)
    load.wait()

    def one(t, carry):
        first = [jnp.zeros((8, HOLD), jnp.float32)] * 2
        second = list(first)
        weights = q.at[pl.ds(pl.multiple_of(t * stations * 8, stations * 8), stations * 8), :]
        for k in range(stations):
            record = table[pl.ds(pl.multiple_of(slot_ref[t, k], 8), 8), :]
            weight = weights[k * 8 : k * 8 + 8, :]
            first[k % 2] += weight * record
            second[k % 2] += weight * pltpu.roll(record, 4, 0)
        acc[pl.ds(pl.multiple_of(t * 16, 16), 8), :] = first[0] + first[1]
        acc[pl.ds(pl.multiple_of(t * 16 + 8, 8), 8), :] = second[0] + second[1]
        return carry

    lax.fori_loop(0, count, one, 0, unroll=4)
    joint = jnp.concatenate(
        [acc[pl.ds(j, count, stride=16), :] + acc[pl.ds(4 + j, count, stride=16), :] for j in range(chunks)]
        + [acc[pl.ds(8 + j, count, stride=16), :] - acc[pl.ds(12 + j, count, stride=16), :] for j in range(chunks)],
        axis=1,
    )
    top = joint.astype(jnp.bfloat16)
    rest = (joint - top.astype(jnp.float32)).astype(jnp.bfloat16)
    parts_ref[:count, :] = top
    parts_ref[count:, :] = rest
    columns = slice(high_ref.shape[1] - early_ref.shape[1], None)
    early_ref[...] = inverse(parts_ref[...], high_ref[:, columns], low_ref[:, columns]).astype(early_ref.dtype)


def detect(slots, blocks, table, q, forward, high, low, count, stations, freqs, time_dev):
    rows = sum(b.shape[0] for b in blocks)
    whole = pl.BlockSpec(memory_space=pltpu.VMEM)
    return pl.pallas_call(
        functools.partial(detect_kernel, len(blocks), count, stations, freqs),
        in_specs=[whole] * (len(blocks) + 6),
        out_specs=[whole] * 3,
        out_shape=[
            jax.ShapeDtypeStruct((2 * count, 2 * freqs), jnp.bfloat16),
            jax.ShapeDtypeStruct((count, time_dev // 2), jnp.bfloat16),
            jax.ShapeDtypeStruct(table.shape, table.dtype),
        ],
        input_output_aliases={1 + len(blocks): 2},
        scratch_shapes=[
            pltpu.VMEM((count * 16, HOLD), jnp.float32),
            pltpu.SMEM(slots.shape, slots.dtype),
            pltpu.SemaphoreType.DMA,
        ],
        compiler_params=pltpu.CompilerParams(vmem_limit_bytes=VMEM_K2),
        cost_estimate=pl.CostEstimate(flops=rows * time_dev * freqs * 4, bytes_accessed=count * stations * 8 * HOLD * 4, transcendentals=0),
        name="detect",
    )(slots, *blocks, table, q, forward, high, low)[:2]


def route(change):
    dx, dz, dc = change
    code = (dx * 4 + dz) * 2 + dc
    return [(i, i ^ code) for i in range(32)]


def position_bits(order):
    return sum((1 + n) << (2 * d) for n, d in enumerate(order))


def per_device(records, templates, channels, moveouts):
    per, time_dev = records.shape
    batches, count, stations, length = templates.shape
    freqs = (time_dev + EXTRA) // 2 + 1
    forward, phase, high, low = (jnp.asarray(t) for t in host_tables(time_dev))
    swap = lambda block, change: lax.ppermute(block, "tmpl", route(change))

    spread = jnp.asarray(spread_table(stations))
    own, waves, head, forward, phase, lags, spread, high, low, slots = load(
        [
            records,
            templates.reshape(-1, length),
            forward[:length],
            forward,
            phase,
            moveouts.reshape(-1, stations),
            spread,
            high,
            low,
        ],
        channels.reshape(-1, stations),
        per,
    )
    line = join([own] + [swap(records, (0, d, 0)) for d in Z_ORDER])
    plane = [swap(line, (d, 0, 0)) for d in X_ORDER]
    q, line_q, table = template_spectra(lags, spread, line, waves, head, forward, phase, 32 * per, freqs)
    far = [swap(block, (0, 0, 1)) for block in [line_q] + plane]
    table = record_spectra(plane + far[:1], forward, table, line.shape[0], freqs)
    parts, early = detect(slots, far[1:], table, q, forward, high, low, batches * count, stations, freqs, time_dev)
    main = own_window(parts, high, low, time_dev)
    earlier = lax.ppermute(early, "tm", [(i, i - 1) for i in range(1, lax.axis_size("tm"))])
    earlier = earlier.astype(jnp.float32)
    out = main + jnp.pad(earlier, ((0, 0), (time_dev - earlier.shape[1], 0)))
    return out.reshape(batches, count, time_dev)


def solution(mesh):
    placed = (
        P("tmpl", "tm"),
        P(None, "tmpl", None, None),
        P(None, "tmpl", None),
        P(None, "tmpl", None),
    )
    return jax.shard_map(
        per_device, mesh=mesh, in_specs=placed, out_specs=P(None, "tmpl", "tm"), check_vma=False
    )
```

```python
import functools
import math

import jax
import jax.numpy as jnp
import numpy as np
from jax import lax
from jax.experimental import pallas as pl
from jax.experimental.pallas import tpu as pltpu
from jax.sharding import PartitionSpec as P

L = 200
LAGS = 56
EXTRA = L + LAGS - 2
HOLD = 128
LAG_ROWS = 64
SPREAD_ROWS = 64
Z_ORDER = (3, 1, 2)
X_ORDER = (2, 1, 3)
VMEM_K1 = 12 << 20
VMEM_K2 = 12 << 20
VMEM_D1 = 4 << 20


def angles(samples, freqs, width):
    return 2.0 * math.pi / width * (samples[:, None] * freqs[None, :] % width)


def host_tables(time_dev):
    width = time_dev + EXTRA
    freqs = width // 2 + 1
    freq = np.arange(freqs)
    ang = angles(np.arange(time_dev), freq, width)
    forward = np.concatenate([np.cos(ang), np.sin(ang)], axis=1).astype(np.float32).astype(jnp.bfloat16)
    turn = angles(np.arange(LAGS), freq, width)
    phase = np.zeros((2 * LAG_ROWS, 2 * freqs), jnp.bfloat16)
    phase[:LAGS], phase[LAG_ROWS : LAG_ROWS + LAGS] = halves(np.concatenate([np.cos(turn), np.sin(turn)], axis=1))
    weight = np.where((freq == 0) | (freq == freqs - 1), 1.0, 2.0) / width
    early = np.arange(time_dev // 2, time_dev) + EXTRA
    tau = np.concatenate([np.arange(time_dev), early])
    back = angles(tau, freq, width)
    inverse = np.concatenate([np.cos(back) * weight, np.sin(back) * weight], axis=1)
    inverse[time_dev:][early < time_dev] = 0.0
    return forward, phase, *halves(inverse.T)


def halves(table):
    table = table.astype(np.float32)
    high = table.astype(jnp.bfloat16)
    return high, (table - high.astype(np.float32)).astype(jnp.bfloat16)


def load_kernel(count, per, *refs):
    sources, (*targets, slot_ref, channel_ref, sems) = refs[:count], refs[count:]
    targets = [channel_ref, *targets]
    copies = [pltpu.make_async_copy(src, dst, sems.at[n]) for n, (src, dst) in enumerate(zip(sources, targets))]
    for copy in copies:
        copy.start()
    copies[0].wait()
    channel = channel_ref[...]
    owner = (channel * reciprocal(per)) >> 16
    apart = owner ^ lax.axis_index("tmpl")
    rank_z = (position_bits(Z_ORDER) >> (apart & 6)) & 3
    rank_x = (position_bits(X_ORDER) >> ((apart >> 2) & 6)) & 3
    slot_ref[...] = (((apart & 1) * 16 + rank_x * 4 + rank_z) * per + channel - owner * per) * 8
    for copy in copies[1:]:
        copy.wait()


def reciprocal(per):
    m = (1 << 16) // per + 1
    n = np.arange(32 * per)
    assert (n * m >> 16 == n // per).all()
    return m


def load(arrays, channels, per):
    whole = pl.BlockSpec(memory_space=pltpu.VMEM)
    return pl.pallas_call(
        functools.partial(load_kernel, len(arrays) + 1, per),
        in_specs=[pl.BlockSpec(memory_space=pltpu.HBM)] * (len(arrays) + 1),
        out_specs=[whole] * (len(arrays) + 1),
        out_shape=[jax.ShapeDtypeStruct(a.shape, a.dtype) for a in (*arrays, channels)],
        scratch_shapes=[pltpu.VMEM(channels.shape, channels.dtype), pltpu.SemaphoreType.DMA((len(arrays) + 1,))],
        compiler_params=pltpu.CompilerParams(vmem_limit_bytes=12 << 20),
        name="load",
    )(*(pltpu.with_memory_space_constraint(a, pltpu.HBM) for a in (channels, *arrays)))


def spread_table(stations):
    at = np.arange(8 * stations)
    spread = np.zeros((SPREAD_ROWS + 16, 8 * stations), jnp.bfloat16)
    spread[at % stations, at] = 1
    spread[SPREAD_ROWS + at // stations, at] = 1
    return spread


def template_kernel(step, freqs, lag_ref, spread_ref, line_ref, waves, head, forward, phases, out, line_out, table):
    line_out[...] = line_ref[...]
    stations = lag_ref.shape[1]
    lags = lag_ref[...].astype(jnp.float32).astype(jnp.bfloat16)
    lags = jnp.dot(lags, spread_ref[:stations, :], preferred_element_type=jnp.float32)
    stretch = spread_ref[pl.ds(SPREAD_ROWS, 8), :].astype(jnp.float32)
    lag_row = (lax.broadcasted_iota(jnp.int32, (2 * LAG_ROWS, step), 0) & (LAG_ROWS - 1)).astype(jnp.float32)
    for start in range(0, waves.shape[0], step):
        group = start // stations
        lag = jnp.sum(lags[group : group + 8] * stretch, axis=0, keepdims=True)
        chosen = (lag_row == lag).astype(jnp.float32).astype(jnp.bfloat16)
        phase = lax.dot_general(chosen, phases[...], (((0,), (0,)), ((), ())), preferred_element_type=jnp.float32)
        dft = jnp.dot(waves[pl.ds(start, step), :], head[...], preferred_element_type=jnp.float32)
        for j in range(freqs // HOLD):
            low, high = slice(j * HOLD, (j + 1) * HOLD), slice(freqs + j * HOLD, freqs + (j + 1) * HOLD)
            h_cos, h_sin, c_theta, s_theta = dft[:, low], dft[:, high], phase[:, low], phase[:, high]
            out[pl.ds(start * 8 + j, step, stride=8), :] = h_cos * c_theta - h_sin * s_theta
            out[pl.ds(start * 8 + 4 + j, step, stride=8), :] = h_cos * s_theta + h_sin * c_theta
    fill_table([line_ref], forward, table, 0, freqs)


def template_spectra(lags, spread, line, waves, head, forward, phase, rows, freqs):
    count, length = waves.shape
    whole = pl.BlockSpec(memory_space=pltpu.VMEM)
    return pl.pallas_call(
        functools.partial(template_kernel, 8 * lags.shape[1], freqs),
        in_specs=[whole] * 7,
        out_specs=[whole] * 3,
        out_shape=[
            jax.ShapeDtypeStruct((count * 8, HOLD), jnp.float32),
            jax.ShapeDtypeStruct(line.shape, line.dtype),
            jax.ShapeDtypeStruct((rows * 8, HOLD), jnp.float32),
        ],
        compiler_params=pltpu.CompilerParams(vmem_limit_bytes=VMEM_K1),
        cost_estimate=pl.CostEstimate(flops=count * length * freqs * 4, bytes_accessed=count * 8 * HOLD * 4, transcendentals=0),
        name="template_spectra",
    )(lags, spread, line, waves, head, forward, phase)


def join_kernel(*refs):
    *parts, out = refs
    at = 0
    for part in parts:
        out[pl.ds(at, part.shape[0]), :] = part[...]
        at += part.shape[0]


def join(parts):
    rows = sum(part.shape[0] for part in parts)
    whole = pl.BlockSpec(memory_space=pltpu.VMEM)
    return pl.pallas_call(
        join_kernel,
        in_specs=[whole] * len(parts),
        out_specs=whole,
        out_shape=jax.ShapeDtypeStruct((rows, parts[0].shape[1]), parts[0].dtype),
        compiler_params=pltpu.CompilerParams(vmem_limit_bytes=2 << 20),
        name="join",
    )(*parts)


def fill_table(blocks, forward_ref, table, first, freqs):
    for b, block in enumerate(blocks):
        size = block.shape[0]
        dft = jnp.dot(block[...], forward_ref[...], preferred_element_type=jnp.float32)
        for j in range(freqs // HOLD):
            start = (first + b * size) * 8 + j
            table[pl.ds(start, size, stride=8), :] = dft[:, j * HOLD : (j + 1) * HOLD]
            table[pl.ds(start + 4, size, stride=8), :] = dft[:, freqs + j * HOLD : freqs + (j + 1) * HOLD]


def record_kernel(freqs, first, *refs):
    *blocks, far_line, far_next, forward_ref, _, table = refs
    fill_table(blocks, forward_ref, table, first, freqs)
    fill_table([far_line, far_next], forward_ref, table, table.shape[0] // 16, freqs)


def record_spectra(blocks, forward, table, first, freqs):
    rows = sum(b.shape[0] for b in blocks)
    whole = pl.BlockSpec(memory_space=pltpu.VMEM)
    return pl.pallas_call(
        functools.partial(record_kernel, freqs, first),
        in_specs=[whole] * (len(blocks) + 2),
        out_specs=whole,
        out_shape=jax.ShapeDtypeStruct(table.shape, table.dtype),
        input_output_aliases={len(blocks) + 1: 0},
        compiler_params=pltpu.CompilerParams(vmem_limit_bytes=VMEM_D1),
        cost_estimate=pl.CostEstimate(flops=rows * forward.shape[0] * freqs * 4, bytes_accessed=rows * 8 * HOLD * 4, transcendentals=0),
        name="record_spectra",
    )(*blocks, forward, table)


def inverse(parts, high, low):
    count = parts.shape[0] // 2
    both = jnp.dot(parts, high, preferred_element_type=jnp.float32)
    return both[:count] + both[count:] + jnp.dot(parts[:count], low, preferred_element_type=jnp.float32)


def inverse_kernel(parts_ref, high_ref, low_ref, main_ref):
    columns = slice(0, main_ref.shape[1])
    main_ref[...] = inverse(parts_ref[...], high_ref[:, columns], low_ref[:, columns])


def own_window(parts, high, low, time_dev):
    whole = pl.BlockSpec(memory_space=pltpu.VMEM)
    count = parts.shape[0] // 2
    return pl.pallas_call(
        inverse_kernel,
        in_specs=[whole] * 3,
        out_specs=whole,
        out_shape=jax.ShapeDtypeStruct((count, time_dev), jnp.float32),
        compiler_params=pltpu.CompilerParams(vmem_limit_bytes=VMEM_D1),
        cost_estimate=pl.CostEstimate(flops=6 * count * parts.shape[1] * time_dev, bytes_accessed=1 << 22, transcendentals=0),
        name="own_window",
    )(parts, high, low)


def detect_kernel(n_blocks, count, stations, freqs, slots, *refs):
    blocks, (_, q, forward_ref, high_ref, low_ref, parts_ref, early_ref, table, acc, slot_ref, sem) = refs[:n_blocks], refs[n_blocks:]
    load = pltpu.make_async_copy(slots, slot_ref, sem)
    load.start()
    chunks = freqs // HOLD
    fill_table(blocks, forward_ref, table, table.shape[0] // 8 - n_blocks * blocks[0].shape[0], freqs)
    load.wait()

    def one(t, carry):
        first = [jnp.zeros((8, HOLD), jnp.float32)] * 2
        second = list(first)
        weights = q.at[pl.ds(pl.multiple_of(t * stations * 8, stations * 8), stations * 8), :]
        for k in range(stations):
            record = table[pl.ds(pl.multiple_of(slot_ref[t, k], 8), 8), :]
            weight = weights[k * 8 : k * 8 + 8, :]
            first[k % 2] += weight * record
            second[k % 2] += weight * pltpu.roll(record, 4, 0)
        acc[pl.ds(pl.multiple_of(t * 16, 16), 8), :] = first[0] + first[1]
        acc[pl.ds(pl.multiple_of(t * 16 + 8, 8), 8), :] = second[0] + second[1]
        return carry

    lax.fori_loop(0, count, one, 0, unroll=4)
    joint = jnp.concatenate(
        [acc[pl.ds(j, count, stride=16), :] + acc[pl.ds(4 + j, count, stride=16), :] for j in range(chunks)]
        + [acc[pl.ds(8 + j, count, stride=16), :] - acc[pl.ds(12 + j, count, stride=16), :] for j in range(chunks)],
        axis=1,
    )
    top = joint.astype(jnp.bfloat16)
    rest = (joint - top.astype(jnp.float32)).astype(jnp.bfloat16)
    parts_ref[:count, :] = top
    parts_ref[count:, :] = rest
    columns = slice(high_ref.shape[1] - early_ref.shape[1], None)
    early_ref[...] = inverse(parts_ref[...], high_ref[:, columns], low_ref[:, columns]).astype(early_ref.dtype)


def detect(slots, blocks, table, q, forward, high, low, count, stations, freqs, time_dev):
    rows = sum(b.shape[0] for b in blocks)
    whole = pl.BlockSpec(memory_space=pltpu.VMEM)
    return pl.pallas_call(
        functools.partial(detect_kernel, len(blocks), count, stations, freqs),
        in_specs=[whole] * (len(blocks) + 6),
        out_specs=[whole] * 3,
        out_shape=[
            jax.ShapeDtypeStruct((2 * count, 2 * freqs), jnp.bfloat16),
            jax.ShapeDtypeStruct((count, time_dev // 2), jnp.bfloat16),
            jax.ShapeDtypeStruct(table.shape, table.dtype),
        ],
        input_output_aliases={1 + len(blocks): 2},
        scratch_shapes=[
            pltpu.VMEM((count * 16, HOLD), jnp.float32),
            pltpu.SMEM(slots.shape, slots.dtype),
            pltpu.SemaphoreType.DMA,
        ],
        compiler_params=pltpu.CompilerParams(vmem_limit_bytes=VMEM_K2),
        cost_estimate=pl.CostEstimate(flops=rows * time_dev * freqs * 4, bytes_accessed=count * stations * 8 * HOLD * 4, transcendentals=0),
        name="detect",
    )(slots, *blocks, table, q, forward, high, low)[:2]


def route(change):
    dx, dz, dc = change
    code = (dx * 4 + dz) * 2 + dc
    return [(i, i ^ code) for i in range(32)]


def position_bits(order):
    return sum((1 + n) << (2 * d) for n, d in enumerate(order))


def per_device(records, templates, channels, moveouts):
    per, time_dev = records.shape
    batches, count, stations, length = templates.shape
    freqs = (time_dev + EXTRA) // 2 + 1
    forward, phase, high, low = (jnp.asarray(t) for t in host_tables(time_dev))
    swap = lambda block, change: lax.ppermute(block, "tmpl", route(change))

    spread = jnp.asarray(spread_table(stations))
    own, waves, head, forward, phase, lags, spread, high, low, slots = load(
        [
            records,
            templates.reshape(-1, length),
            forward[:length],
            forward,
            phase,
            moveouts.reshape(-1, stations),
            spread,
            high,
            low,
        ],
        channels.reshape(-1, stations),
        per,
    )
    line = join([own] + [swap(records, (0, d, 0)) for d in Z_ORDER])
    plane = [swap(line, (d, 0, 0)) for d in X_ORDER]
    q, line_q, table = template_spectra(lags, spread, line, waves, head, forward, phase, 32 * per, freqs)
    far = [swap(block, (0, 0, 1)) for block in [line_q] + plane]
    table = record_spectra(plane + far[:2], forward, table, line.shape[0], freqs)
    parts, early = detect(slots, far[2:], table, q, forward, high, low, batches * count, stations, freqs, time_dev)
    main = own_window(parts, high, low, time_dev)
    earlier = lax.ppermute(early, "tm", [(i, i - 1) for i in range(1, lax.axis_size("tm"))])
    earlier = earlier.astype(jnp.float32)
    out = main + jnp.pad(earlier, ((0, 0), (time_dev - earlier.shape[1], 0)))
    return out.reshape(batches, count, time_dev)


def solution(mesh):
    placed = (
        P("tmpl", "tm"),
        P(None, "tmpl", None, None),
        P(None, "tmpl", None),
        P(None, "tmpl", None),
    )
    return jax.shard_map(
        per_device, mesh=mesh, in_specs=placed, out_specs=P(None, "tmpl", "tm"), check_vma=False
    )
```
